512 devices in a mesh: dp: 32 (over x, y), seq: 16 (over z, core).
Axes of the slice: x: 4, y: 8, z: 8, core: 2. Of those that a mesh axis runs over, the one named last changes fastest.
Arguments:
- mixer_input: bfloat16 [32, 2048, 2048], P('dp', 'seq'), may hold values from -5 to 5
- state_input: bfloat16 [32, 2048, 256], P('dp', 'seq'), may hold values from -1 to 1
- step_raw: float32 [32, 32, 2048], P('dp', None, 'seq'), may hold values from -5 to 6
- conv_weight: float32 [4, 2304], replicated, may hold values from -3 to 3
- conv_bias: float32 [2304], replicated, may hold values from -0.3 to 0.3
- step_bias: float32 [32], replicated, may hold values from -0.5 to 0.5
- log_rate: float32 [32], replicated, may hold values from -10 to -1
- skip_gain: float32 [32], replicated, may hold values from 0.25 to 1.75
- grad_out: bfloat16 [32, 2048, 2048], P('dp', 'seq'), may hold values from -6 to 6
Outputs:
- grad_mixer: bfloat16 [32, 2048, 2048], P('dp', 'seq')
- grad_state: bfloat16 [32, 2048, 256], P('dp', 'seq')
- grad_step: float32 [32, 32, 2048], P('dp', None, 'seq')
- grad_conv_weight: float32 [4, 2304], replicated
- grad_conv_bias: float32 [2304], replicated
- grad_step_bias: float32 [32], replicated
- grad_log_rate: float32 [32], replicated
- grad_skip_gain: float32 [32], replicated
The draws below stay inside these ranges and needn't reach their ends.
All inputs are finite; a program needn't handle non-finite values.
Results may differ from the reference program's by a relative error of at most 0.013.
Values may be sent and summed in bfloat16 or wider, within the bound.
No kernel may reach another device: no remote copies, remote signals or barrier semaphores. Data moves between devices by JAX's collectives and lax.ppermute only.
A program may use at most 128 MiB of HBM per device.

```python
import math
import jax
import jax.numpy as jnp
from jax import lax

HALF_ATTENDERS = 32
HEAD_DIM = 64
STATE = 128
CONV = 4
SHARD_LOCATIONS = 128
INNER = 2048
CHANNELS = 2304
SERIES_EXTENT = 2048
SERIES_COUNT = 32
N_SEQ = 16


def head_plan(key):
    plan_key = jax.random.fold_in(key, 7)
    pick_key, fast_key, middle_key, slow_key = jax.random.split(plan_key, 4)
    picked = jax.random.randint(pick_key, (HALF_ATTENDERS,), 0, 16)
    fast_heads = picked < 4
    middle_heads = (picked >= 4) & (picked < 8)
    block_loss = jnp.exp(jax.random.uniform(fast_key, (HALF_ATTENDERS,), jnp.float32, math.log(2.5), math.log(4.5)))
    middle_loss = jnp.exp(jax.random.uniform(middle_key, (HALF_ATTENDERS,), jnp.float32, math.log(0.1), math.log(0.2)))
    chain_loss = jnp.exp(jax.random.uniform(slow_key, (HALF_ATTENDERS,), jnp.float32, math.log(0.3), math.log(0.8)))
    quick_heads = fast_heads | middle_heads
    quick_rate = block_loss / SHARD_LOCATIONS
    slow_rate = chain_loss / (SERIES_EXTENT * 0.095)
    fading_quickness = jnp.where(quick_heads, quick_rate, slow_rate)
    base_step = jnp.where(fast_heads, 1.0, jnp.where(middle_heads, middle_loss / block_loss, 0.095))
    return (fading_quickness, base_step)


def draw_log_rate(key, part):
    fading_quickness, base_step = head_plan(key)
    return jnp.log(fading_quickness)


def draw_step_raw(key, part):
    fading_quickness, base_step = head_plan(key)
    personal_seed = jax.random.fold_in(key, 19)
    section_seed, jagged_seed, beginning_seed, spike_seed = jax.random.split(personal_seed, 4)
    draw_shape = (SERIES_COUNT, HALF_ATTENDERS, SERIES_EXTENT)
    block_count = SERIES_EXTENT // SHARD_LOCATIONS
    block_factor = jnp.exp(jax.random.uniform(section_seed, (SERIES_COUNT, HALF_ATTENDERS, block_count), jnp.float32, -0.4, 0.4))
    block_factor = jnp.repeat(block_factor, SHARD_LOCATIONS, axis=2)
    rough_factor = jnp.exp(0.3 * jnp.clip(jax.random.normal(jagged_seed, draw_shape, jnp.float32), -1.5, 1.5))
    baseline_amplitude = base_step[None, :, None] * block_factor * rough_factor
    spike_beginnings = jax.random.randint(beginning_seed, (SERIES_COUNT, 3), 0, SERIES_EXTENT - SHARD_LOCATIONS + 1)
    location_lattice = jnp.arange(SERIES_EXTENT)[None, None, :]
    inside_spike = jnp.any((location_lattice >= spike_beginnings[:, :, None]) & (location_lattice < spike_beginnings[:, :, None] + SHARD_LOCATIONS), axis=1)
    spike_surcharge = jnp.exp(jax.random.uniform(spike_seed, (SERIES_COUNT, HALF_ATTENDERS), jnp.float32, math.log(0.2), math.log(0.45)))
    spike_addition = spike_surcharge / (fading_quickness[None, :] * SHARD_LOCATIONS)
    stride_durations = baseline_amplitude + jnp.where(inside_spike[:, None, :], spike_addition[:, :, None], 0.0)
    return jnp.clip(jnp.log(jnp.expm1(stride_durations)), -5.0, 6.0)


def draw_mixer_input(key, part):
    value_key = jax.random.fold_in(jax.random.fold_in(key, 23), 0)
    draw_shape = (SERIES_COUNT, SERIES_EXTENT, INNER)
    values = jnp.clip(jax.random.normal(value_key, draw_shape, jnp.float32), -5.0, 5.0)
    return values.astype(jnp.bfloat16)


def draw_state_input(key, part):
    value_key = jax.random.fold_in(jax.random.fold_in(key, 29), 0)
    draw_shape = (SERIES_COUNT, SERIES_EXTENT, 2 * STATE)
    values = jnp.clip(0.2 * jax.random.normal(value_key, draw_shape, jnp.float32), -1.0, 1.0)
    return values.astype(jnp.bfloat16)


def levels(key, extent, shards, smallest, top_value):
    factor_of = 1.0
    for position, parts in shards:
        steps = jax.random.uniform(jax.random.fold_in(jax.random.fold_in(key, 6), position), (parts,), jnp.float32, smallest / len(shards), top_value / len(shards))
        factor_of = factor_of * jnp.repeat(jnp.exp(steps), extent[position] // parts).reshape((-1,) + (1,) * (len(extent) - 1 - position))
    return factor_of


def scatter_about(own_key, dims, deviation, limit, shards=(), kind=jnp.bfloat16):
    array = jax.random.normal(own_key, dims, jnp.float32) * deviation
    if len(shards) > 0:
        array = levels(own_key, dims, shards, -0.22, 0.18) * array
    return jnp.clip(array, min=-limit, max=limit).astype(kind)


def setup_inputs(seed: int = 0) -> dict:
    arg_keys = jax.random.split(jax.random.key(seed), 10)
    return {
        "mixer_input": draw_mixer_input(jax.random.fold_in(arg_keys[9], 71), 0),
        "state_input": draw_state_input(jax.random.fold_in(arg_keys[9], 71), 0),
        "step_raw": draw_step_raw(jax.random.fold_in(arg_keys[9], 71), 0),
        "conv_weight": scatter_about(arg_keys[3], (CONV, CHANNELS), CONV ** -0.5, 3.0, (), jnp.float32),
        "conv_bias": scatter_about(arg_keys[4], (CHANNELS,), 0.05, 0.3, (), jnp.float32),
        "step_bias": jnp.clip(jax.random.uniform(arg_keys[5], (HALF_ATTENDERS,), jnp.float32, -0.5, 0.5), -0.5, 0.5),
        "log_rate": draw_log_rate(jax.random.fold_in(arg_keys[9], 71), 0),
        "skip_gain": jnp.clip(1.0 + 0.15 * jax.random.normal(arg_keys[7], (HALF_ATTENDERS,), jnp.float32), 0.25, 1.75),
        "grad_out": scatter_about(arg_keys[8], (SERIES_COUNT, SERIES_EXTENT, INNER), 1.0, 6.0, ((0, 32), (1, 16))),
    }


highest = lax.Precision.HIGHEST

def convolve(padded, weight, offset):
    kernel_taps = weight.shape[0]
    row_count = padded.shape[0] - kernel_taps + 1
    wide = padded.astype(jnp.float32)
    summed = offset[None, :] + weight[0][None, :] * wide[0:row_count]
    for tap_index in range(1, kernel_taps):
        summed = summed + weight[tap_index][None, :] * wide[tap_index:tap_index + row_count]
    return jax.nn.silu(summed).astype(jnp.bfloat16)

def prepare(padded_x, padded_bc, step_block, conv_weight, conv_bias, step_bias, log_rate):
    inner_width = padded_x.shape[1]
    state_width = padded_bc.shape[1] // 2
    x_active = convolve(padded_x, conv_weight[:, :inner_width], conv_bias[:inner_width])
    bc_active = convolve(padded_bc, conv_weight[:, inner_width:], conv_bias[inner_width:])
    b_active = bc_active[:, :state_width]
    c_active = bc_active[:, state_width:]
    stride_durations = jax.nn.softplus(step_block + step_bias[:, None])
    log_decay = -jnp.exp(log_rate)[:, None] * stride_durations
    cumul = jnp.cumsum(log_decay, axis=1)
    return (x_active, b_active, c_active, stride_durations, cumul)

def end_state(x_active, b_active, stride_durations, cumul, head_count):
    row_count = x_active.shape[0]
    weights = jnp.exp(cumul[:, -1:] - cumul) * stride_durations
    scaled = (x_active.astype(jnp.float32).reshape(row_count, head_count, -1) * weights.T[:, :, None]).astype(jnp.bfloat16)
    return jnp.einsum('shp,sn->hpn', scaled.astype(jnp.float32), b_active.astype(jnp.float32), precision=highest)

def block_forward(padded_x, padded_bc, step_block, conv_weight, conv_bias, step_bias, log_rate, skip_gain, entry_state):
    head_count = step_block.shape[0]
    x_active, b_active, c_active, stride_durations, cumul = prepare(padded_x, padded_bc, step_block, conv_weight, conv_bias, step_bias, log_rate)
    row_count = x_active.shape[0]
    scores = jnp.dot(c_active, b_active.T, preferred_element_type=jnp.float32)
    causal = jnp.arange(row_count)[:, None] >= jnp.arange(row_count)[None, :]
    log_gap = jnp.where(causal[None], cumul[:, :, None] - cumul[:, None, :], -jnp.inf)
    mixing = (scores[None] * jnp.exp(log_gap) * stride_durations[:, None, :]).astype(jnp.bfloat16)
    x_heads = x_active.reshape(row_count, head_count, -1)
    inner_out = jnp.einsum('hts,shp->thp', mixing.astype(jnp.float32), x_heads.astype(jnp.float32), precision=highest)
    carried = jnp.einsum('tn,hpn->thp', c_active.astype(jnp.float32), entry_state, precision=highest) * jnp.exp(cumul).T[:, :, None]
    output = inner_out + carried + skip_gain[None, :, None] * x_heads.astype(jnp.float32)
    finish = jnp.exp(cumul[:, -1])[:, None, None] * entry_state + end_state(x_active, b_active, stride_durations, cumul, head_count)
    return (output.reshape(row_count, -1), finish)

def record_forward(x_rec, bc_rec, step_rec, conv_weight, conv_bias, step_bias, log_rate, skip_gain):
    kernel_taps = conv_weight.shape[0]
    x_pad = jnp.concatenate([jnp.zeros((kernel_taps - 1, x_rec.shape[1]), x_rec.dtype), x_rec], 0)
    bc_pad = jnp.concatenate([jnp.zeros((kernel_taps - 1, bc_rec.shape[1]), bc_rec.dtype), bc_rec], 0)
    head_count = step_rec.shape[0]
    zero_state = jnp.zeros((head_count, HEAD_DIM, STATE), jnp.float32)

    def one_block(running, block_index):
        first_row = (block_index * SHARD_LOCATIONS).astype(jnp.int32)
        x_block = lax.dynamic_slice_in_dim(x_pad, first_row, SHARD_LOCATIONS + kernel_taps - 1, 0)
        bc_block = lax.dynamic_slice_in_dim(bc_pad, first_row, SHARD_LOCATIONS + kernel_taps - 1, 0)
        step_block = lax.dynamic_slice_in_dim(step_rec, first_row, SHARD_LOCATIONS, 1)
        output, next_state = block_forward(x_block, bc_block, step_block, conv_weight, conv_bias, step_bias, log_rate, skip_gain, running)
        return (next_state, output)
    last_state, block_outputs = lax.scan(one_block, zero_state, jnp.arange(N_SEQ, dtype=jnp.int32))
    return block_outputs.reshape(N_SEQ * SHARD_LOCATIONS, -1)

def reference(mixer_input, state_input, step_raw, conv_weight, conv_bias, step_bias, log_rate, skip_gain, grad_out):

    def per_record(record_items):
        x_rec, bc_rec, step_rec, cotangent = record_items
        output, pull_back = jax.vjp(record_forward, x_rec, bc_rec, step_rec, conv_weight, conv_bias, step_bias, log_rate, skip_gain)
        return pull_back(cotangent.astype(jnp.float32))
    gradients = lax.map(per_record, (mixer_input, state_input, step_raw, grad_out))
    return (gradients[0], gradients[1], gradients[2], lax.optimization_barrier(jnp.sum(gradients[3], 0)) / SERIES_COUNT, lax.optimization_barrier(jnp.sum(gradients[4], 0)) / SERIES_COUNT, lax.optimization_barrier(jnp.sum(gradients[5], 0)) / SERIES_COUNT, lax.optimization_barrier(jnp.sum(gradients[6], 0)) / SERIES_COUNT, lax.optimization_barrier(jnp.sum(gradients[7], 0)) / SERIES_COUNT)
```

```python
import jax
import jax.numpy as jnp
from jax import lax
from jax.experimental import pallas as pl
from jax.experimental.pallas import tpu as pltpu
from jax.sharding import PartitionSpec as P

HIGH = lax.Precision.HIGHEST
F32 = jnp.float32
BF16 = jnp.bfloat16
ROWS = 128
LANES = 128
HALO = 8
VMEM = pl.BlockSpec(memory_space=pltpu.VMEM)
SMEM = pl.BlockSpec(memory_space=pltpu.SMEM)
INTERPRET = False


def call(body, outs, ins, scratch=()):
    return pl.pallas_call(
        body,
        out_shape=outs,
        in_specs=ins,
        out_specs=[VMEM] * len(outs),
        scratch_shapes=list(scratch),
        interpret=INTERPRET,
    )


def shape(*dims, dtype=F32):
    return jax.ShapeDtypeStruct(dims, dtype)


def dot(a, b, dims=((1,), (0,)), precision=None):
    return lax.dot_general(
        a, b, (dims, ((), ())), precision=precision, preferred_element_type=F32
    )


NT = ((1,), (1,))
TN = ((0,), (0,))


def iota(dims, axis):
    return lax.broadcasted_iota(jnp.int32, dims, axis)


def column_of(ref, count):
    rows = iota((count, LANES), 0)
    col = jnp.zeros((count, LANES), F32)
    for h in range(count):
        col = jnp.where(rows == h, ref[h], col)
    return col


def steps_body(step_ref, bias_ref, rate_ref, rows_ref, cols_ref):
    heads = step_ref.shape[0]
    raw = step_ref[...] + column_of(bias_ref, heads)
    step = jnp.maximum(raw, 0.0) + jnp.log1p(jnp.exp(-jnp.abs(raw)))
    rate = -jnp.exp(column_of(rate_ref, heads))
    upto = (iota((ROWS, ROWS), 0) <= iota((ROWS, ROWS), 1)).astype(F32)
    cumul = dot(rate * step, upto, precision=HIGH)
    weight = jnp.exp(cumul[:, ROWS - 1 :] - cumul) * step
    fade = jnp.exp(cumul)
    stack = jnp.concatenate([cumul, step, weight, fade], 0)
    rows_ref[: 4 * heads, :] = stack
    rows_ref[4 * heads : 5 * heads, :] = jax.nn.sigmoid(raw)
    rows_ref[5 * heads :, :] = rate
    cols_ref[...] = stack.T


def preact(ext_ref, taps_ref, at, lanes):
    acc = taps_ref[4:5, pl.ds(at, lanes)]
    for k in range(4):
        acc = acc + taps_ref[k : k + 1, pl.ds(at, lanes)] * ext_ref[pl.ds(HALO - 3 + k, ROWS), :]
    return acc


def pair_column(cols_ref, first, second, left):
    a = jnp.broadcast_to(cols_ref[:, first : first + 1], (ROWS, LANES))
    b = jnp.broadcast_to(cols_ref[:, second : second + 1], (ROWS, LANES))
    return jnp.where(left, a, b)


def first_body(x_ref, bc_ref, halo_ref, taps_ref, g_ref, cols_ref, xact_ref, bcact_ref, send_ref, ext_ref, ext2_ref):
    inner = x_ref.shape[1]
    heads = inner // 64
    ext2_ref[:HALO, :] = halo_ref[:, inner:].astype(F32)
    ext2_ref[HALO:, :] = bc_ref[...].astype(F32)
    pre = preact(ext2_ref, taps_ref, inner, 2 * LANES)
    bc = (pre * jax.nn.sigmoid(pre)).astype(BF16)
    bcact_ref[...] = bc
    b_t = bc[:, :LANES].astype(F32).T.astype(BF16)
    c_t = bc[:, LANES:].astype(F32).T.astype(BF16)
    left = iota((ROWS, LANES), 1) < 64
    for i in range(inner // LANES):
        at = i * LANES
        lanes = pl.ds(at, LANES)
        ext = ext_ref.at[i % 2]
        ext[:HALO, :] = halo_ref[:, lanes].astype(F32)
        ext[HALO:, :] = x_ref[:, lanes].astype(F32)
        pre = preact(ext, taps_ref, at, LANES)
        act = (pre * jax.nn.sigmoid(pre)).astype(BF16)
        xact_ref[:, lanes] = act
        weight = pair_column(cols_ref, 2 * heads + 2 * i, 2 * heads + 2 * i + 1, left)
        fade = pair_column(cols_ref, 3 * heads + 2 * i, 3 * heads + 2 * i + 1, left)
        xw = (act.astype(F32) * weight).astype(BF16)
        gw = (g_ref[:, lanes].astype(F32) * fade).astype(BF16)
        send_ref[i, :ROWS, :] = dot(b_t, xw).astype(BF16)
        send_ref[i, ROWS : 2 * ROWS, :] = dot(c_t, gw).astype(BF16)
        total = fade[ROWS - 1 :, :]
        high = total.astype(BF16)
        low = (total - high.astype(F32)).astype(BF16)
        row = iota((16, LANES), 0)
        send_ref[i, 2 * ROWS :, :] = jnp.where(row == 0, high.astype(F32), jnp.where(row == 1, low.astype(F32), 0.0)).astype(BF16)


def scan_body(got_ref, out_ref):
    count = got_ref.shape[0]

    def decay(j):
        tail = got_ref[j, 2 * ROWS :, :].astype(F32)
        return tail[0:1, :] + tail[1:2, :]

    state = jnp.zeros((ROWS, LANES), F32)
    for j in range(count):
        out_ref[j, :ROWS, :] = state.astype(BF16)
        state = decay(j) * state + got_ref[j, :ROWS, :].astype(F32)
    state = jnp.zeros((ROWS, LANES), F32)
    for j in range(count - 1, -1, -1):
        out_ref[j, ROWS:, :] = state.astype(BF16)
        state = decay(j) * state + got_ref[j, ROWS : 2 * ROWS, :].astype(F32)


def inner_body(
    x_ref, bc_ref, halo_ref, taps_ref, g_ref, rows_ref, cols_ref, xact_ref, bcact_ref, skip_ref,
    dx_ref, slope_ref, xw_ref, gw_ref, dbc_ref, slope2_ref, row_ref, ext_ref, ext2_ref,
):
    inner = x_ref.shape[1]
    heads = inner // 64
    ext2_ref[:HALO, :] = halo_ref[:, inner:].astype(F32)
    ext2_ref[HALO:, :] = bc_ref[...].astype(F32)
    pre = preact(ext2_ref, taps_ref, inner, 2 * LANES)
    gate = jax.nn.sigmoid(pre)
    slope2_ref[...] = gate * (1.0 + pre * (1.0 - gate))
    b = bcact_ref[:, :LANES]
    c = bcact_ref[:, LANES:]
    scores = dot(b, c, NT)
    causal = iota((ROWS, ROWS), 0) <= iota((ROWS, ROWS), 1)
    left = iota((ROWS, LANES), 1) < 64
    ones = jnp.ones((8, ROWS), BF16)
    dscores = jnp.zeros((ROWS, ROWS), F32)
    for i in range(inner // LANES):
        at = i * LANES
        lanes = pl.ds(at, LANES)
        ext = ext_ref.at[i % 2]
        ext[:HALO, :] = halo_ref[:, lanes].astype(F32)
        ext[HALO:, :] = x_ref[:, lanes].astype(F32)
        pre = preact(ext, taps_ref, at, LANES)
        gate = jax.nn.sigmoid(pre)
        slope_ref[:, lanes] = gate * (1.0 + pre * (1.0 - gate))
        act = xact_ref[:, lanes]
        g = g_ref[:, lanes]
        wide = g.astype(F32)
        weight = pair_column(cols_ref, 2 * heads + 2 * i, 2 * heads + 2 * i + 1, left)
        fade = pair_column(cols_ref, 3 * heads + 2 * i, 3 * heads + 2 * i + 1, left)
        xw_ref[:, lanes] = (act.astype(F32) * weight).astype(BF16)
        gw_ref[:, lanes] = (wide * fade).astype(BF16)
        skip = jnp.where(left, skip_ref[2 * i], skip_ref[2 * i + 1])
        dx = skip * wide
        both = jnp.sum(act.astype(F32) * wide, 0, keepdims=True)
        row_ref[2 * heads + 2 * i : 2 * heads + 2 * i + 1, :] = jnp.where(left[:1], both, 0.0)
        row_ref[2 * heads + 2 * i + 1 : 2 * heads + 2 * i + 2, :] = jnp.where(left[:1], 0.0, both)
        for k in range(2):
            h = 2 * i + k
            mine = left if k == 0 else ~left
            own = jnp.where(mine, wide, 0.0).astype(BF16)
            gap = rows_ref[h : h + 1, :] - cols_ref[:, h : h + 1]
            fall = jnp.exp(jnp.where(causal, gap, -1e30)) * cols_ref[:, heads + h : heads + h + 1]
            mixing = scores * fall
            dmix = dot(act, own, NT).astype(BF16).astype(F32)
            dscores = dscores + dmix * fall
            both = (dmix * mixing).astype(BF16)
            row_ref[h : h + 1, :] = dot(ones, both)[:1]
            row_ref[heads + h : heads + h + 1, :] = dot(ones, both, NT)[:1]
            dx = dx + dot(mixing.astype(BF16), own)
        dx_ref[:, lanes] = dx
    ds = dscores.astype(BF16)
    dbc_ref[:, :LANES] = dot(ds, c)
    dbc_ref[:, LANES:] = dot(ds, b, TN)


def back_through(dact, slope, pad_ref, ext_ref, taps_ref, at, lanes, out_ref, out_at, rim_ref):
    dpre = dact.astype(BF16).astype(F32) * slope
    pad_ref[:HALO, :] = jnp.zeros((HALO, lanes), F32)
    pad_ref[HALO : HALO + ROWS, :] = dpre
    pad_ref[HALO + ROWS :, :] = jnp.zeros((HALO, lanes), F32)
    own = jnp.zeros((ROWS, lanes), F32)
    rim = jnp.zeros((HALO, lanes), F32)
    sums = []
    for k in range(4):
        tap = taps_ref[k : k + 1, pl.ds(at, lanes)]
        own = own + tap * pad_ref[pl.ds(HALO + 3 - k, ROWS), :]
        rim = rim + tap * pad_ref[pl.ds(HALO - k, HALO), :]
        sums.append(jnp.sum(dpre * ext_ref[pl.ds(HALO - 3 + k, ROWS), :], 0, keepdims=True))
    sums.append(jnp.sum(dpre, 0, keepdims=True))
    out_ref[:, pl.ds(out_at, lanes)] = own.astype(BF16)
    rim_ref[:, pl.ds(at, lanes)] = rim.astype(BF16)
    return sums


def last_body(
    x_ref, bc_ref, halo_ref, taps_ref, rows_ref, cols_ref, bcact_ref, states_ref,
    dx_ref, slope_ref, xw_ref, gw_ref, dbc_ref, slope2_ref, row_ref,
    gx_ref, gbc_ref, gstep_ref, rim_ref, part_ref, ext_ref, pad_ref, ext2_ref, pad2_ref, acc_ref,
):
    inner = x_ref.shape[1]
    heads = inner // 64
    b = bcact_ref[:, :LANES]
    c = bcact_ref[:, LANES:]
    left = iota((ROWS, LANES), 1) < 64
    half = jnp.where((iota((8, LANES), 1) < 64) == (iota((8, LANES), 0) == 0), 1.0, 0.0).astype(BF16)
    db = dbc_ref[:, :LANES]
    dc = dbc_ref[:, LANES:]
    part_ref[...] = jnp.zeros(part_ref.shape, F32)
    for i in range(inner // LANES):
        at = i * LANES
        lanes = pl.ds(at, LANES)
        state = states_ref[i, :ROWS, :]
        later = states_ref[i, ROWS:, :]
        xw = xw_ref[:, lanes]
        gw = gw_ref[:, lanes]
        carried = dot(c, state) * gw.astype(F32)
        dxw = dot(b, later).astype(BF16).astype(F32)
        dc = dc + dot(gw, state, NT)
        db = db + dot(xw, later, NT)
        acc_ref[2 * i : 2 * i + 2, :] = dot(half, carried.astype(BF16), NT)[:2]
        acc_ref[heads + 2 * i : heads + 2 * i + 2, :] = dot(half, (dxw * xw.astype(F32)).astype(BF16), NT)[:2]
        both = jnp.sum(state.astype(F32) * later.astype(F32), 0, keepdims=True)
        acc_ref[2 * heads + 2 * i : 2 * heads + 2 * i + 1, :] = jnp.where(left[:1], both, 0.0)
        acc_ref[2 * heads + 2 * i + 1 : 2 * heads + 2 * i + 2, :] = jnp.where(left[:1], 0.0, both)
        weight = pair_column(cols_ref, 2 * heads + 2 * i, 2 * heads + 2 * i + 1, left)
        ext = ext_ref.at[i % 2]
        ext[:HALO, :] = halo_ref[:, lanes].astype(F32)
        ext[HALO:, :] = x_ref[:, lanes].astype(F32)
        sums = back_through(
            dx_ref[:, lanes] + weight * dxw, slope_ref[:, lanes], pad_ref.at[i % 2], ext, taps_ref, at, LANES, gx_ref, at, rim_ref
        )
        for k in range(5):
            part_ref[i, k : k + 1, :] = sums[k]
    ext2_ref[:HALO, :] = halo_ref[:, inner:].astype(F32)
    ext2_ref[HALO:, :] = bc_ref[...].astype(F32)
    dbc = jnp.concatenate([db, dc], 1)
    sums = back_through(dbc, slope2_ref[...], pad2_ref, ext2_ref, taps_ref, inner, 2 * LANES, gbc_ref, 0, rim_ref)
    for k in range(5):
        part_ref[k, 5:6, :] = sums[k][:, :LANES]
        part_ref[k, 6:7, :] = sums[k][:, LANES:]
    step = rows_ref[heads : 2 * heads, :]
    gate = rows_ref[4 * heads : 5 * heads, :]
    rate = rows_ref[5 * heads : 6 * heads, :]
    total = rows_ref[3 * heads : 4 * heads, ROWS - 1 :]
    at_t = row_ref[:heads, :]
    at_s = row_ref[heads : 2 * heads, :]
    ended = acc_ref[heads : 2 * heads, :]
    at_end = jnp.sum(ended, 1, keepdims=True) + total * jnp.sum(acc_ref[2 * heads : 3 * heads, :], 1, keepdims=True)
    final = iota((heads, ROWS), 1) == ROWS - 1
    dcumul = at_t - at_s + acc_ref[:heads, :] - ended + jnp.where(final, at_end, 0.0)
    onward = (iota((ROWS, ROWS), 0) >= iota((ROWS, ROWS), 1)).astype(F32)
    ddecay = dot(dcumul, onward, precision=HIGH)
    dstep = (at_s + ended) / step + ddecay * rate
    dstep = dstep * gate
    gstep_ref[...] = dstep
    dbias = jnp.sum(dstep, 1, keepdims=True)
    drate = jnp.sum(ddecay * rate * step, 1, keepdims=True)
    dskip = jnp.sum(row_ref[2 * heads : 3 * heads, :], 1, keepdims=True)
    r, l = iota((heads, LANES), 0), iota((heads, LANES), 1)
    placed = jnp.where(l == r, dbias, jnp.where(l == r + heads, drate, jnp.where(l == r + 2 * heads, dskip, 0.0)))
    part_ref[0, 7:8, :] = jnp.sum(placed, 0, keepdims=True)


def on_device(
    mixer_input, state_input, step_raw, conv_weight, conv_bias, step_bias, log_rate, skip_gain, grad_out
):
    x, bc, step, g = mixer_input[0], state_input[0], step_raw[0], grad_out[0]
    rows, inner = x.shape
    heads = step.shape[0]
    pairs = inner // LANES
    n_seq, n_dp = lax.axis_size("seq"), lax.axis_size("dp")
    assert rows == ROWS and n_seq == pairs and bc.shape[1] == 2 * LANES and heads * 64 == inner
    tail = jnp.concatenate([x[rows - HALO :], bc[rows - HALO :]], 1)
    halo = lax.ppermute(tail, "seq", [(i, i + 1) for i in range(n_seq - 1)])
    taps = jnp.concatenate([conv_weight, conv_bias[None]], 0)
    by_row, by_col = call(
        steps_body, [shape(6 * heads, ROWS), shape(ROWS, 4 * heads)], [VMEM, SMEM, SMEM]
    )(step, step_bias, log_rate)
    ext = [pltpu.VMEM((2, ROWS + HALO, LANES), F32)]
    ext2 = [pltpu.VMEM((ROWS + HALO, 2 * LANES), F32)]
    x_act, bc_act, send = call(
        first_body,
        [shape(rows, inner, dtype=BF16), shape(rows, 2 * LANES, dtype=BF16), shape(pairs, 2 * ROWS + 16, LANES, dtype=BF16)],
        [VMEM] * 6,
        ext + ext2,
    )(x, bc, halo, taps, g, by_col)
    got = lax.all_to_all(send, "seq", 0, 0)
    dx, slope, xw, gw, dbc, slope2, row = call(
        inner_body,
        [
            shape(rows, inner),
            shape(rows, inner),
            shape(rows, inner, dtype=BF16),
            shape(rows, inner, dtype=BF16),
            shape(rows, 2 * LANES),
            shape(rows, 2 * LANES),
            shape(3 * heads, ROWS),
        ],
        [VMEM] * 9 + [SMEM],
        ext + ext2,
    )(x, bc, halo, taps, g, by_row, by_col, x_act, bc_act, skip_gain)
    scanned = call(scan_body, [shape(n_seq, 2 * ROWS, LANES, dtype=BF16)], [VMEM])(got)[0]
    states = lax.all_to_all(scanned, "seq", 0, 0)
    gx, gbc, gstep, rim, part = call(
        last_body,
        [
            shape(rows, inner, dtype=BF16),
            shape(rows, 2 * LANES, dtype=BF16),
            shape(heads, ROWS),
            shape(HALO, inner + 2 * LANES, dtype=BF16),
            shape(pairs, 8, LANES),
        ],
        [VMEM] * 15,
        ext
        + [pltpu.VMEM((2, ROWS + 2 * HALO, LANES), F32)]
        + ext2
        + [pltpu.VMEM((ROWS + 2 * HALO, 2 * LANES), F32), pltpu.VMEM((3 * heads, ROWS), F32)],
    )(x, bc, halo, taps, by_row, by_col, bc_act, states, dx, slope, xw, gw, dbc, slope2, row)
    back = lax.ppermute(rim, "seq", [(i, i - 1) for i in range(1, n_seq)])
    mine = jnp.sum(lax.all_to_all(part, "seq", 0, 0), 0)
    shared = lax.all_to_all(jnp.broadcast_to(mine[None], (n_dp, 8, LANES)), "dp", 0, 0)
    mean = jnp.sum(shared, 0) / n_dp
    whole = lax.all_to_all(jnp.broadcast_to(mean[None], (pairs, 8, LANES)), "seq", 0, 0)
    gx = gx.at[rows - 3 :].add(back[:3, :inner])
    gbc = gbc.at[rows - 3 :].add(back[:3, inner:])
    conv = jnp.concatenate([whole[:, k, :].reshape(1, inner) for k in range(5)], 0)
    conv = jnp.concatenate([conv, whole[:5, 5, :], whole[:5, 6, :]], 1)
    small = whole[0, 7]
    return (
        gx[None],
        gbc[None],
        gstep[None],
        conv[:4],
        conv[4],
        small[:heads],
        small[heads : 2 * heads],
        small[2 * heads : 3 * heads],
    )


def solution(mesh):
    return jax.shard_map(
        on_device,
        mesh=mesh,
        in_specs=(
            P("dp", "seq", None),
            P("dp", "seq", None),
            P("dp", None, "seq"),
            P(),
            P(),
            P(),
            P(),
            P(),
            P("dp", "seq", None),
        ),
        out_specs=(
            P("dp", "seq", None),
            P("dp", "seq", None),
            P("dp", None, "seq"),
            P(),
            P(),
            P(),
            P(),
            P(),
        ),
        check_vma=False,
    )
```

```python
import jax
import jax.numpy as jnp
from jax import lax
from jax.experimental import pallas as pl
from jax.experimental.pallas import tpu as pltpu
from jax.sharding import PartitionSpec as P

HIGH = lax.Precision.HIGHEST
F32 = jnp.float32
BF16 = jnp.bfloat16
ROWS = 128
LANES = 128
HALO = 8
VMEM = pl.BlockSpec(memory_space=pltpu.VMEM)
FAR = pl.BlockSpec(memory_space=pltpu.VMEM)
SMEM = pl.BlockSpec(memory_space=pltpu.SMEM)
INTERPRET = False


def call(body, outs, ins, scratch=()):
    kernel = pl.pallas_call(
        body,
        out_shape=outs,
        in_specs=ins,
        out_specs=[VMEM] * len(outs),
        scratch_shapes=list(scratch),
        compiler_params=pltpu.CompilerParams(vmem_limit_bytes=16 << 20),
        interpret=INTERPRET,
    )
    if INTERPRET:
        return kernel
    return lambda *given: kernel(
        *(
            pltpu.with_memory_space_constraint(a, pltpu.VMEM if spec is VMEM else pltpu.HBM)
            for a, spec in zip(given, ins, strict=True)
        )
    )


def shape(*dims, dtype=F32):
    return jax.ShapeDtypeStruct(dims, dtype)


def kept(*dims, dtype=F32):
    return shape(*dims, dtype=dtype) if INTERPRET else pltpu.VMEM(dims, dtype)


def dot(a, b, dims=((1,), (0,)), precision=None):
    return lax.dot_general(
        a, b, (dims, ((), ())), precision=precision, preferred_element_type=F32
    )


NT = ((1,), (1,))
TN = ((0,), (0,))


def iota(dims, axis):
    return lax.broadcasted_iota(jnp.int32, dims, axis)


def column_of(ref, count):
    rows = iota((count, LANES), 0)
    col = jnp.zeros((count, LANES), F32)
    for h in range(count):
        col = jnp.where(rows == h, ref[h], col)
    return col


def steps_body(step_ref, weight_ref, offset_ref, bias_ref, rate_ref, rows_ref, cols_ref, taps_ref):
    heads = step_ref.shape[0]
    taps_ref[:4, :] = weight_ref[...]
    taps_ref[4:5, :] = offset_ref[...].reshape(1, -1)
    raw = step_ref[...] + column_of(bias_ref, heads)
    step = jnp.maximum(raw, 0.0) + jnp.log1p(jnp.exp(-jnp.abs(raw)))
    rate = -jnp.exp(column_of(rate_ref, heads))
    upto = (iota((ROWS, ROWS), 0) <= iota((ROWS, ROWS), 1)).astype(F32)
    cumul = dot(rate * step, upto, precision=HIGH)
    weight = jnp.exp(cumul[:, ROWS - 1 :] - cumul) * step
    fade = jnp.exp(cumul)
    stack = jnp.concatenate([cumul, step, weight, fade], 0)
    rows_ref[: 4 * heads, :] = stack
    rows_ref[4 * heads : 5 * heads, :] = jax.nn.sigmoid(raw)
    rows_ref[5 * heads :, :] = rate
    cols_ref[...] = stack.T


def preact(ext_ref, taps_ref, at, lanes):
    acc = taps_ref[4:5, pl.ds(at, lanes)]
    for k in range(4):
        acc = acc + taps_ref[k : k + 1, pl.ds(at, lanes)] * ext_ref[pl.ds(HALO - 3 + k, ROWS), :]
    return acc


def pair_column(cols_ref, first, second, left):
    a = jnp.broadcast_to(cols_ref[:, first : first + 1], (ROWS, LANES))
    b = jnp.broadcast_to(cols_ref[:, second : second + 1], (ROWS, LANES))
    return jnp.where(left, a, b)


def first_body(x_ref, bc_ref, halo_ref, taps_ref, g_ref, cols_ref, bcact_ref, send_ref, ext_ref, ext2_ref):
    inner = x_ref.shape[1]
    heads = inner // 64
    ext2_ref[:HALO, :] = halo_ref[:, inner:].astype(F32)
    ext2_ref[HALO:, :] = bc_ref[...].astype(F32)
    pre = preact(ext2_ref, taps_ref, inner, 2 * LANES)
    bc = (pre * jax.nn.sigmoid(pre)).astype(BF16)
    bcact_ref[...] = bc
    b_t = bc[:, :LANES].astype(F32).T.astype(BF16)
    c_t = bc[:, LANES:].astype(F32).T.astype(BF16)
    left = iota((ROWS, LANES), 1) < 64
    for i in range(inner // LANES):
        at = i * LANES
        lanes = pl.ds(at, LANES)
        ext = ext_ref.at[i % 2]
        ext[:HALO, :] = halo_ref[:, lanes].astype(F32)
        ext[HALO:, :] = x_ref[:, lanes].astype(F32)
        pre = preact(ext, taps_ref, at, LANES)
        act = (pre * jax.nn.sigmoid(pre)).astype(BF16)
        weight = pair_column(cols_ref, 2 * heads + 2 * i, 2 * heads + 2 * i + 1, left)
        fade = pair_column(cols_ref, 3 * heads + 2 * i, 3 * heads + 2 * i + 1, left)
        xw = (act.astype(F32) * weight).astype(BF16)
        gw = (g_ref[:, lanes].astype(F32) * fade).astype(BF16)
        send_ref[i % 2, i // 2, :ROWS, :] = dot(b_t, xw).astype(BF16)
        send_ref[i % 2, i // 2, ROWS : 2 * ROWS, :] = dot(c_t, gw).astype(BF16)
        total = fade[ROWS - 1 :, :]
        send_ref[i % 2, i // 2, 2 * ROWS :, :] = decay_rows(total)


def decay_of(tail):
    tail = tail.astype(F32)
    return tail[0:1, :] + tail[1:2, :]


def decay_rows(total):
    high = total.astype(BF16).astype(F32)
    row = iota((16, LANES), 0)
    return jnp.where(row == 0, high, jnp.where(row == 1, total - high, 0.0)).astype(BF16)


def join_body(got_ref, out_ref):
    for i in range(got_ref.shape[1]):
        first, second = decay_of(got_ref[0, i, 2 * ROWS :, :]), decay_of(got_ref[1, i, 2 * ROWS :, :])
        end = second * got_ref[0, i, :ROWS, :].astype(F32) + got_ref[1, i, :ROWS, :].astype(F32)
        by_entry = got_ref[0, i, ROWS : 2 * ROWS, :].astype(F32) + first * got_ref[1, i, ROWS : 2 * ROWS, :].astype(F32)
        out_ref[i, :ROWS, :] = end.astype(BF16)
        out_ref[i, ROWS : 2 * ROWS, :] = by_entry.astype(BF16)
        out_ref[i, 2 * ROWS :, :] = decay_rows(first * second)


def scan_body(got_ref, out_ref):
    count = got_ref.shape[0]
    state = jnp.zeros((ROWS, LANES), F32)
    for j in range(count):
        out_ref[j, :ROWS, :] = state.astype(BF16)
        state = decay_of(got_ref[j, 2 * ROWS :, :]) * state + got_ref[j, :ROWS, :].astype(F32)
    state = jnp.zeros((ROWS, LANES), F32)
    for j in range(count - 1, -1, -1):
        out_ref[j, ROWS:, :] = state.astype(BF16)
        state = decay_of(got_ref[j, 2 * ROWS :, :]) * state + got_ref[j, ROWS : 2 * ROWS, :].astype(F32)


def part_body(got_ref, both_ref, out_ref):
    for i in range(both_ref.shape[0]):
        state, later = both_ref[i, :ROWS, :], both_ref[i, ROWS:, :]
        first, second = decay_of(got_ref[0, i, 2 * ROWS :, :]), decay_of(got_ref[1, i, 2 * ROWS :, :])
        out_ref[0, i, :ROWS, :] = state
        out_ref[1, i, :ROWS, :] = (first * state.astype(F32) + got_ref[0, i, :ROWS, :].astype(F32)).astype(BF16)
        out_ref[0, i, ROWS:, :] = (second * later.astype(F32) + got_ref[1, i, ROWS : 2 * ROWS, :].astype(F32)).astype(BF16)
        out_ref[1, i, ROWS:, :] = later


def inner_body(
    x_ref, bc_ref, halo_ref, taps_ref, g_ref, rows_ref, cols_ref, bcact_ref, skip_ref,
    dx_ref, slope_ref, xw_ref, gw_ref, dbc_ref, slope2_ref, row_ref, ext_ref, ext2_ref,
):
    inner = x_ref.shape[1]
    heads = inner // 64
    ext2_ref[:HALO, :] = halo_ref[:, inner:].astype(F32)
    ext2_ref[HALO:, :] = bc_ref[...].astype(F32)
    pre = preact(ext2_ref, taps_ref, inner, 2 * LANES)
    gate = jax.nn.sigmoid(pre)
    slope2_ref[...] = gate * (1.0 + pre * (1.0 - gate))
    b = bcact_ref[:, :LANES]
    c = bcact_ref[:, LANES:]
    scores = dot(b, c, NT)
    causal = iota((ROWS, ROWS), 0) <= iota((ROWS, ROWS), 1)
    left = iota((ROWS, LANES), 1) < 64
    ones = jnp.ones((8, ROWS), BF16)
    dscores = jnp.zeros((ROWS, ROWS), F32)
    for i in range(inner // LANES):
        at = i * LANES
        lanes = pl.ds(at, LANES)
        ext = ext_ref.at[i % 2]
        ext[:HALO, :] = halo_ref[:, lanes].astype(F32)
        ext[HALO:, :] = x_ref[:, lanes].astype(F32)
        pre = preact(ext, taps_ref, at, LANES)
        gate = jax.nn.sigmoid(pre)
        slope_ref[:, lanes] = gate * (1.0 + pre * (1.0 - gate))
        act = (pre * gate).astype(BF16)
        g = g_ref[:, lanes]
        wide = g.astype(F32)
        weight = pair_column(cols_ref, 2 * heads + 2 * i, 2 * heads + 2 * i + 1, left)
        fade = pair_column(cols_ref, 3 * heads + 2 * i, 3 * heads + 2 * i + 1, left)
        xw_ref[:, lanes] = (act.astype(F32) * weight).astype(BF16)
        gw_ref[:, lanes] = (wide * fade).astype(BF16)
        skip = jnp.where(left, skip_ref[2 * i], skip_ref[2 * i + 1])
        dx = skip * wide
        both = jnp.sum(act.astype(F32) * wide, 0, keepdims=True)
        row_ref[2 * heads + 2 * i : 2 * heads + 2 * i + 1, :] = jnp.where(left[:1], both, 0.0)
        row_ref[2 * heads + 2 * i + 1 : 2 * heads + 2 * i + 2, :] = jnp.where(left[:1], 0.0, both)
        for k in range(2):
            h = 2 * i + k
            mine = left if k == 0 else ~left
            own = jnp.where(mine, wide, 0.0).astype(BF16)
            gap = rows_ref[h : h + 1, :] - cols_ref[:, h : h + 1]
            fall = jnp.exp(jnp.where(causal, gap, -1e30)) * cols_ref[:, heads + h : heads + h + 1]
            mixing = scores * fall
            dmix = dot(act, own, NT).astype(BF16).astype(F32)
            dscores = dscores + dmix * fall
            both = (dmix * mixing).astype(BF16)
            row_ref[h : h + 1, :] = dot(ones, both)[:1]
            row_ref[heads + h : heads + h + 1, :] = dot(ones, both, NT)[:1]
            dx = dx + dot(mixing.astype(BF16), own)
        dx_ref[:, lanes] = dx
    ds = dscores.astype(BF16)
    dbc_ref[:, :LANES] = dot(ds, c)
    dbc_ref[:, LANES:] = dot(ds, b, TN)


def back_through(dact, slope, pad_ref, ext_ref, taps_ref, at, lanes, out_ref, out_at, rim_ref):
    dpre = dact.astype(BF16).astype(F32) * slope
    pad_ref[:HALO, :] = jnp.zeros((HALO, lanes), F32)
    pad_ref[HALO : HALO + ROWS, :] = dpre
    pad_ref[HALO + ROWS :, :] = jnp.zeros((HALO, lanes), F32)
    own = jnp.zeros((ROWS, lanes), F32)
    rim = jnp.zeros((HALO, lanes), F32)
    sums = []
    for k in range(4):
        tap = taps_ref[k : k + 1, pl.ds(at, lanes)]
        own = own + tap * pad_ref[pl.ds(HALO + 3 - k, ROWS), :]
        rim = rim + tap * pad_ref[pl.ds(HALO - k, HALO), :]
        sums.append(jnp.sum(dpre * ext_ref[pl.ds(HALO - 3 + k, ROWS), :], 0, keepdims=True))
    sums.append(jnp.sum(dpre, 0, keepdims=True))
    out_ref[:, pl.ds(out_at, lanes)] = own.astype(BF16)
    rim_ref[:, pl.ds(at, lanes)] = rim.astype(BF16)
    return sums


def last_body(
    x_ref, bc_ref, halo_ref, taps_ref, rows_ref, cols_ref, bcact_ref, states_ref,
    dx_ref, slope_ref, xw_ref, gw_ref, dbc_ref, slope2_ref, row_ref,
    gx_ref, gbc_ref, gstep_ref, rim_ref, part_ref, ext_ref, pad_ref, ext2_ref, pad2_ref, acc_ref,
):
    inner = x_ref.shape[1]
    heads = inner // 64
    b = bcact_ref[:, :LANES]
    c = bcact_ref[:, LANES:]
    left = iota((ROWS, LANES), 1) < 64
    half = jnp.where((iota((8, LANES), 1) < 64) == (iota((8, LANES), 0) == 0), 1.0, 0.0).astype(BF16)
    db = dbc_ref[:, :LANES]
    dc = dbc_ref[:, LANES:]
    part_ref[...] = jnp.zeros(part_ref.shape, F32)
    for i in range(inner // LANES):
        at = i * LANES
        lanes = pl.ds(at, LANES)
        state = states_ref[i % 2, i // 2, :ROWS, :]
        later = states_ref[i % 2, i // 2, ROWS:, :]
        xw = xw_ref[:, lanes]
        gw = gw_ref[:, lanes]
        carried = dot(c, state) * gw.astype(F32)
        dxw = dot(b, later).astype(BF16).astype(F32)
        dc = dc + dot(gw, state, NT)
        db = db + dot(xw, later, NT)
        acc_ref[2 * i : 2 * i + 2, :] = dot(half, carried.astype(BF16), NT)[:2]
        acc_ref[heads + 2 * i : heads + 2 * i + 2, :] = dot(half, (dxw * xw.astype(F32)).astype(BF16), NT)[:2]
        both = jnp.sum(state.astype(F32) * later.astype(F32), 0, keepdims=True)
        acc_ref[2 * heads + 2 * i : 2 * heads + 2 * i + 1, :] = jnp.where(left[:1], both, 0.0)
        acc_ref[2 * heads + 2 * i + 1 : 2 * heads + 2 * i + 2, :] = jnp.where(left[:1], 0.0, both)
        weight = pair_column(cols_ref, 2 * heads + 2 * i, 2 * heads + 2 * i + 1, left)
        ext = ext_ref.at[i % 2]
        ext[:HALO, :] = halo_ref[:, lanes].astype(F32)
        ext[HALO:, :] = x_ref[:, lanes].astype(F32)
        sums = back_through(
            dx_ref[:, lanes] + weight * dxw, slope_ref[:, lanes], pad_ref.at[i % 2], ext, taps_ref, at, LANES, gx_ref, at, rim_ref
        )
        for k in range(5):
            part_ref[i, k : k + 1, :] = sums[k]
    ext2_ref[:HALO, :] = halo_ref[:, inner:].astype(F32)
    ext2_ref[HALO:, :] = bc_ref[...].astype(F32)
    dbc = jnp.concatenate([db, dc], 1)
    sums = back_through(dbc, slope2_ref[...], pad2_ref, ext2_ref, taps_ref, inner, 2 * LANES, gbc_ref, 0, rim_ref)
    for k in range(5):
        part_ref[k, 5:6, :] = sums[k][:, :LANES]
        part_ref[k, 6:7, :] = sums[k][:, LANES:]
    step = rows_ref[heads : 2 * heads, :]
    gate = rows_ref[4 * heads : 5 * heads, :]
    rate = rows_ref[5 * heads : 6 * heads, :]
    total = rows_ref[3 * heads : 4 * heads, ROWS - 1 :]
    at_t = row_ref[:heads, :]
    at_s = row_ref[heads : 2 * heads, :]
    ended = acc_ref[heads : 2 * heads, :]
    at_end = jnp.sum(ended, 1, keepdims=True) + total * jnp.sum(acc_ref[2 * heads : 3 * heads, :], 1, keepdims=True)
    final = iota((heads, ROWS), 1) == ROWS - 1
    dcumul = at_t - at_s + acc_ref[:heads, :] - ended + jnp.where(final, at_end, 0.0)
    onward = (iota((ROWS, ROWS), 0) >= iota((ROWS, ROWS), 1)).astype(F32)
    ddecay = dot(dcumul, onward, precision=HIGH)
    dstep = (at_s + ended) / step + ddecay * rate
    dstep = dstep * gate
    gstep_ref[...] = dstep
    dbias = jnp.sum(dstep, 1, keepdims=True)
    drate = jnp.sum(ddecay * rate * step, 1, keepdims=True)
    dskip = jnp.sum(row_ref[2 * heads : 3 * heads, :], 1, keepdims=True)
    r, l = iota((heads, LANES), 0), iota((heads, LANES), 1)
    placed = jnp.where(l == r, dbias, jnp.where(l == r + heads, drate, jnp.where(l == r + 2 * heads, dskip, 0.0)))
    part_ref[0, 7:8, :] = jnp.sum(placed, 0, keepdims=True)


def on_device(
    mixer_input, state_input, step_raw, conv_weight, conv_bias, step_bias, log_rate, skip_gain, grad_out
):
    x, bc, step, g = mixer_input[0], state_input[0], step_raw[0], grad_out[0]
    rows, inner = x.shape
    heads = step.shape[0]
    pairs = inner // LANES
    n_seq, n_dp = lax.axis_size("seq"), lax.axis_size("dp")
    assert rows == ROWS and n_seq == pairs and bc.shape[1] == 2 * LANES and heads * 64 == inner
    tail = jnp.concatenate([x[rows - HALO :], bc[rows - HALO :]], 1)
    halo = lax.ppermute(tail, "seq", [(i, i + 1) for i in range(n_seq - 1)])
    by_row, by_col, taps = call(
        steps_body,
        [kept(6 * heads, ROWS), kept(ROWS, 4 * heads), kept(5, inner + 2 * LANES)],
        [FAR, FAR, FAR, SMEM, SMEM],
    )(step, conv_weight, conv_bias, step_bias, log_rate)
    ext = [pltpu.VMEM((2, ROWS + HALO, LANES), F32)]
    ext2 = [pltpu.VMEM((ROWS + HALO, 2 * LANES), F32)]
    bc_act, send = call(
        first_body,
        [kept(rows, 2 * LANES, dtype=BF16), shape(2, pairs // 2, 2 * ROWS + 16, LANES, dtype=BF16)],
        [FAR, FAR, VMEM, VMEM, FAR, VMEM],
        ext + ext2,
    )(x, bc, halo, taps, g, by_col)
    chips = n_seq // 2
    cores = [[2 * c, 2 * c + 1] for c in range(chips)]
    ring = [[2 * c + k for c in range(chips)] for k in range(2)]
    got = lax.all_to_all(send, "seq", 0, 0, axis_index_groups=cores)
    joined = call(join_body, [shape(pairs // 2, 2 * ROWS + 16, LANES, dtype=BF16)], [VMEM])(got)[0]
    joined = lax.all_to_all(joined, "seq", 0, 0, axis_index_groups=ring)
    dx, slope, xw, gw, dbc, slope2, row = call(
        inner_body,
        [
            kept(rows, inner),
            kept(rows, inner),
            kept(rows, inner, dtype=BF16),
            kept(rows, inner, dtype=BF16),
            kept(rows, 2 * LANES),
            kept(rows, 2 * LANES),
            kept(3 * heads, ROWS),
        ],
        [VMEM] * 8 + [SMEM],
        ext + ext2,
    )(x, bc, halo, taps, g, by_row, by_col, bc_act, skip_gain)
    scanned = call(scan_body, [shape(chips, 2 * ROWS, LANES, dtype=BF16)], [VMEM])(joined)[0]
    scanned = lax.all_to_all(scanned, "seq", 0, 0, axis_index_groups=ring)
    parted = call(part_body, [shape(2, chips, 2 * ROWS, LANES, dtype=BF16)], [VMEM] * 2)(got, scanned)[0]
    states = lax.all_to_all(parted, "seq", 0, 0, axis_index_groups=cores)
    gx, gbc, gstep, rim, part = call(
        last_body,
        [
            shape(rows, inner, dtype=BF16),
            shape(rows, 2 * LANES, dtype=BF16),
            shape(heads, ROWS),
            shape(HALO, inner + 2 * LANES, dtype=BF16),
            shape(pairs, 8, LANES),
        ],
        [VMEM] * 15,
        ext
        + [pltpu.VMEM((2, ROWS + 2 * HALO, LANES), F32)]
        + ext2
        + [pltpu.VMEM((ROWS + 2 * HALO, 2 * LANES), F32), pltpu.VMEM((3 * heads, ROWS), F32)],
    )(x, bc, halo, taps, by_row, by_col, bc_act, states, dx, slope, xw, gw, dbc, slope2, row)
    back = lax.ppermute(rim, "seq", [(i, i - 1) for i in range(1, n_seq)])
    mine = jnp.sum(lax.all_to_all(part, "seq", 0, 0), 0)
    shared = lax.all_to_all(jnp.broadcast_to(mine[None], (n_dp, 8, LANES)), "dp", 0, 0)
    mean = jnp.sum(shared, 0) / n_dp
    whole = lax.all_to_all(jnp.broadcast_to(mean[None], (pairs, 8, LANES)), "seq", 0, 0)
    gx = gx.at[rows - 3 :].add(back[:3, :inner])
    gbc = gbc.at[rows - 3 :].add(back[:3, inner:])
    conv = jnp.concatenate([whole[:, k, :].reshape(1, inner) for k in range(5)], 0)
    conv = jnp.concatenate([conv, whole[:5, 5, :], whole[:5, 6, :]], 1)
    small = whole[0, 7]
    return (
        gx[None],
        gbc[None],
        gstep[None],
        conv[:4],
        conv[4],
        small[:heads],
        small[heads : 2 * heads],
        small[2 * heads : 3 * heads],
    )


def solution(mesh):
    return jax.shard_map(
        on_device,
        mesh=mesh,
        in_specs=(
            P("dp", "seq", None),
            P("dp", "seq", None),
            P("dp", None, "seq"),
            P(),
            P(),
            P(),
            P(),
            P(),
            P("dp", "seq", None),
        ),
        out_specs=(
            P("dp", "seq", None),
            P("dp", "seq", None),
            P("dp", None, "seq"),
            P(),
            P(),
            P(),
            P(),
            P(),
        ),
        check_vma=False,
    )
```

```python
import jax
import jax.numpy as jnp
from jax import lax
from jax.experimental import pallas as pl
from jax.experimental.pallas import tpu as pltpu
from jax.sharding import PartitionSpec as P


HIGH = lax.Precision.HIGHEST
F32 = jnp.float32
BF16 = jnp.bfloat16
ROWS = 128
LANES = 128
HALO = 8
PAIRS = 8
HEADS = 16
HALF = PAIRS * LANES
SEG = 2 * ROWS
G_AT, B_AT, C_AT, STEP_AT = HALF, 2 * HALF, 2 * HALF + ROWS, 2 * HALF + 2 * ROWS
SIDE_AT = STEP_AT + 3 * HEADS
PACKED = SIDE_AT + 16
SENT = 2 * ROWS + 16
VMEM = pl.BlockSpec(memory_space=pltpu.VMEM)
FAR = pl.BlockSpec(memory_space=pltpu.VMEM)
SMEM = pl.BlockSpec(memory_space=pltpu.SMEM)
INTERPRET = False
NT = ((1,), (1,))
TN = ((0,), (0,))


def call(body, outs, ins, scratch=()):
    kernel = pl.pallas_call(
        body,
        out_shape=outs,
        in_specs=ins,
        out_specs=[VMEM] * len(outs),
        scratch_shapes=list(scratch),
        compiler_params=pltpu.CompilerParams(vmem_limit_bytes=16 << 20),
        interpret=INTERPRET,
    )
    if INTERPRET:
        return kernel
    return lambda *given: kernel(
        *(
            pltpu.with_memory_space_constraint(a, pltpu.VMEM if spec is VMEM else pltpu.HBM)
            for a, spec in zip(given, ins, strict=True)
        )
    )


def shape(*dims, dtype=F32):
    return jax.ShapeDtypeStruct(dims, dtype)


def far(*dims, dtype=F32):
    return shape(*dims, dtype=dtype) if INTERPRET else pltpu.HBM(dims, dtype)


def kept(*dims, dtype=F32):
    return shape(*dims, dtype=dtype) if INTERPRET else pltpu.VMEM(dims, dtype)


def dot(a, b, dims=((1,), (0,)), precision=None):
    return lax.dot_general(a, b, (dims, ((), ())), precision=precision, preferred_element_type=F32)


def iota(dims, axis):
    return lax.broadcasted_iota(jnp.int32, dims, axis)


def pack_body(x_ref, bc_ref, g_ref, step_ref, out_ref):
    bc = bc_ref[...]
    for q in range(2):
        for o in range(PAIRS):
            at = q * HALF + o * LANES
            out_ref[q, o * ROWS : (o + 1) * ROWS, :] = x_ref[:, at : at + LANES]
            out_ref[q, G_AT + o * ROWS : G_AT + (o + 1) * ROWS, :] = g_ref[:, at : at + LANES]
        out_ref[q, B_AT : B_AT + ROWS, :] = bc[:, :LANES]
        out_ref[q, C_AT : C_AT + ROWS, :] = bc[:, LANES:]
        rest = step_ref[q * HEADS : (q + 1) * HEADS, :]
        for k in range(3):
            piece = rest.astype(BF16)
            rest = rest - piece.astype(F32)
            out_ref[q, STEP_AT + k * HEADS : STEP_AT + (k + 1) * HEADS, :] = piece
        out_ref[q, SIDE_AT:, :] = jnp.full((16, LANES), float(q), F32).astype(BF16)


def tail_body(got_ref, out_ref):
    for o in range(PAIRS):
        out_ref[o, :, :] = got_ref[1, (o + 1) * ROWS - HALO : (o + 1) * ROWS, :]
    out_ref[PAIRS, :, :] = got_ref[1, B_AT + ROWS - HALO : B_AT + ROWS, :]
    out_ref[PAIRS + 1, :, :] = got_ref[1, C_AT + ROWS - HALO : C_AT + ROWS, :]


def head_rows(ref, second):
    rows = iota((2 * HEADS, LANES), 0) % HEADS
    out = jnp.zeros((2 * HEADS, LANES), F32)
    for h in range(HEADS):
        out = jnp.where(rows == h, jnp.where(second, ref[HEADS + h], ref[h]), out)
    return out


def steps_body(got_ref, weight_ref, offset_ref, bias_ref, rate_ref, skip_ref, rows_ref, cols_ref, taps_ref, side_ref):
    side = got_ref[0, SIDE_AT:, :].astype(F32)[:8]
    side_ref[...] = side
    second = side[:1] > 0.5
    offset = offset_ref[...].reshape(1, -1)
    inner = 2 * HALF
    for o in range(PAIRS):
        at = o * LANES
        lanes = slice(at, at + LANES)
        other = slice(HALF + at, HALF + at + LANES)
        taps_ref[:4, lanes] = jnp.where(second, weight_ref[:, other], weight_ref[:, lanes])
        taps_ref[4:5, lanes] = jnp.where(second, offset[:, other], offset[:, lanes])
    taps_ref[:4, HALF:] = weight_ref[:, inner:]
    taps_ref[4:5, HALF:] = offset[:, inner:]
    n = 2 * HEADS
    raw = [
        sum(got_ref[r, STEP_AT + k * HEADS : STEP_AT + (k + 1) * HEADS, :].astype(F32) for k in (2, 1, 0)) for r in range(2)
    ]
    second = jnp.broadcast_to(second, (n, LANES))
    raw = jnp.concatenate(raw, 0) + head_rows(bias_ref, second)
    step = jnp.maximum(raw, 0.0) + jnp.log1p(jnp.exp(-jnp.abs(raw)))
    rate = -jnp.exp(head_rows(rate_ref, second))
    upto = (iota((ROWS, ROWS), 0) <= iota((ROWS, ROWS), 1)).astype(F32)
    cumul = dot(rate * step, upto, precision=HIGH)
    weight = jnp.exp(cumul[:, ROWS - 1 :] - cumul) * step
    fade = jnp.exp(cumul)
    stack = jnp.concatenate([cumul, step, weight, fade], 0)
    rows_ref[: 4 * n, :] = stack
    rows_ref[4 * n : 5 * n, :] = jax.nn.sigmoid(raw)
    rows_ref[5 * n : 6 * n, :] = rate
    rows_ref[6 * n :, :] = head_rows(skip_ref, second)
    cols_ref[...] = stack.T


def head_of(r, o):
    return r * HEADS + 2 * o


def fill(ext_ref, halo, first, second):
    ext_ref[:HALO, :] = halo.astype(F32)
    ext_ref[HALO : HALO + ROWS, :] = first.astype(F32)
    ext_ref[HALO + ROWS :, :] = second.astype(F32)


def fill_pair(ext_ref, got_ref, halo_ref, o):
    rows = slice(o * ROWS, (o + 1) * ROWS)
    fill(ext_ref, halo_ref[o], got_ref[0, rows, :], got_ref[1, rows, :])


def fill_bc(ext2_ref, got_ref, halo_ref):
    for k, at in enumerate((B_AT, C_AT)):
        lanes = slice(k * LANES, (k + 1) * LANES)
        fill(ext2_ref.at[:, lanes], halo_ref[PAIRS + k], got_ref[0, at : at + ROWS, :], got_ref[1, at : at + ROWS, :])


def preact(ext_ref, taps_ref, at, lanes):
    acc = taps_ref[4:5, at : at + lanes]
    for k in range(4):
        acc = acc + taps_ref[k : k + 1, at : at + lanes] * ext_ref[pl.ds(HALO - 3 + k, SEG), :]
    return acc


def pair_column(cols_ref, which, r, o, left):
    at = which * 2 * HEADS + head_of(r, o)
    a = jnp.broadcast_to(cols_ref[:, at : at + 1], (ROWS, LANES))
    b = jnp.broadcast_to(cols_ref[:, at + 1 : at + 2], (ROWS, LANES))
    return jnp.where(left, a, b)


def decay_of(tail):
    tail = tail.astype(F32)
    return tail[0:1, :] + tail[1:2, :]


def decay_rows(total):
    high = total.astype(BF16).astype(F32)
    row = iota((16, LANES), 0)
    return jnp.where(row == 0, high, jnp.where(row == 1, total - high, 0.0)).astype(BF16)


def first_body(got_ref, halo_ref, taps_ref, cols_ref, bcact_ref, near_ref, send_ref, ext_ref, ext2_ref):
    fill_bc(ext2_ref, got_ref, halo_ref)
    pre = preact(ext2_ref, taps_ref, HALF, 2 * LANES)
    bc = pre * jax.nn.sigmoid(pre)
    bcact_ref[...] = bc.astype(BF16)
    bc = bc.astype(BF16).astype(F32)
    b_t = [bc[r * ROWS : (r + 1) * ROWS, :LANES].T.astype(BF16) for r in range(2)]
    c_t = [bc[r * ROWS : (r + 1) * ROWS, LANES:].T.astype(BF16) for r in range(2)]
    left = iota((ROWS, LANES), 1) < 64
    for o in range(PAIRS):
        ext = ext_ref.at[o % 2]
        fill_pair(ext, got_ref, halo_ref, o)
        pre = preact(ext, taps_ref, o * LANES, LANES)
        act = (pre * jax.nn.sigmoid(pre)).astype(BF16).astype(F32)
        ends, backs, totals = [], [], []
        for r in range(2):
            fade = pair_column(cols_ref, 3, r, o, left)
            xw = (act[r * ROWS : (r + 1) * ROWS] * pair_column(cols_ref, 2, r, o, left)).astype(BF16)
            gw = (got_ref[r, G_AT + o * ROWS : G_AT + (o + 1) * ROWS, :].astype(F32) * fade).astype(BF16)
            ends.append(dot(b_t[r], xw))
            backs.append(dot(c_t[r], gw))
            totals.append(fade[ROWS - 1 :, :])
        near_ref[o, :ROWS, :] = ends[0].astype(BF16)
        near_ref[o, ROWS:, :] = backs[1].astype(BF16)
        send_ref[o, :ROWS, :] = (totals[1] * ends[0] + ends[1]).astype(BF16)
        send_ref[o, ROWS : 2 * ROWS, :] = (backs[0] + totals[0] * backs[1]).astype(BF16)
        send_ref[o, 2 * ROWS :, :] = decay_rows(totals[0] * totals[1])


def scan_body(got_ref, out_ref):
    count = got_ref.shape[0]
    state = jnp.zeros((ROWS, LANES), F32)
    for j in range(count):
        out_ref[j, :ROWS, :] = state.astype(BF16)
        state = decay_of(got_ref[j, 2 * ROWS :, :]) * state + got_ref[j, :ROWS, :].astype(F32)
    state = jnp.zeros((ROWS, LANES), F32)
    for j in range(count - 1, -1, -1):
        out_ref[j, ROWS:, :] = state.astype(BF16)
        state = decay_of(got_ref[j, 2 * ROWS :, :]) * state + got_ref[j, ROWS : 2 * ROWS, :].astype(F32)


def inner_body(
    got_ref, halo_ref, taps_ref, rows_ref, cols_ref, bcact_ref,
    dx_ref, slope_ref, xw_ref, gw_ref, dbc_ref, slope2_ref, row_ref, ext_ref, ext2_ref,
):
    n = 2 * HEADS
    fill_bc(ext2_ref, got_ref, halo_ref)
    pre = preact(ext2_ref, taps_ref, HALF, 2 * LANES)
    gate = jax.nn.sigmoid(pre)
    slope2_ref[...] = gate * (1.0 + pre * (1.0 - gate))
    causal = iota((ROWS, ROWS), 0) <= iota((ROWS, ROWS), 1)
    left = iota((ROWS, LANES), 1) < 64
    ones = jnp.ones((8, ROWS), BF16)
    b = [bcact_ref[r * ROWS : (r + 1) * ROWS, :LANES] for r in range(2)]
    c = [bcact_ref[r * ROWS : (r + 1) * ROWS, LANES:] for r in range(2)]
    scores = [dot(b[r], c[r], NT) for r in range(2)]
    dscores = [jnp.zeros((ROWS, ROWS), F32) for _ in range(2)]
    for o in range(PAIRS):
        ext = ext_ref.at[o % 2]
        fill_pair(ext, got_ref, halo_ref, o)
        pre = preact(ext, taps_ref, o * LANES, LANES)
        gate = jax.nn.sigmoid(pre)
        slope_ref[o] = gate * (1.0 + pre * (1.0 - gate))
        whole = (pre * gate).astype(BF16)
        for r in range(2):
            h = head_of(r, o)
            rows = slice(r * ROWS, (r + 1) * ROWS)
            act = whole[rows]
            wide = got_ref[r, G_AT + o * ROWS : G_AT + (o + 1) * ROWS, :].astype(F32)
            xw_ref[o, rows] = (act.astype(F32) * pair_column(cols_ref, 2, r, o, left)).astype(BF16)
            gw_ref[o, rows] = (wide * pair_column(cols_ref, 3, r, o, left)).astype(BF16)
            skip = jnp.where(left[:1], rows_ref[6 * n + h : 6 * n + h + 1, :], rows_ref[6 * n + h + 1 : 6 * n + h + 2, :])
            dx = skip * wide
            both = jnp.sum(act.astype(F32) * wide, 0, keepdims=True)
            row_ref[2 * n + h : 2 * n + h + 1, :] = jnp.where(left[:1], both, 0.0)
            row_ref[2 * n + h + 1 : 2 * n + h + 2, :] = jnp.where(left[:1], 0.0, both)
            for k in range(2):
                own = jnp.where(left if k == 0 else ~left, wide, 0.0).astype(BF16)
                gap = rows_ref[h + k : h + k + 1, :] - cols_ref[:, h + k : h + k + 1]
                fall = jnp.exp(jnp.where(causal, gap, -1e30)) * cols_ref[:, n + h + k : n + h + k + 1]
                mixing = scores[r] * fall
                dmix = dot(act, own, NT).astype(BF16).astype(F32)
                dscores[r] = dscores[r] + dmix * fall
                both = (dmix * mixing).astype(BF16)
                row_ref[h + k : h + k + 1, :] = dot(ones, both)[:1]
                row_ref[n + h + k : n + h + k + 1, :] = dot(ones, both, NT)[:1]
                dx = dx + dot(mixing.astype(BF16), own)
            dx_ref[o, rows] = dx
    for r in range(2):
        ds = dscores[r].astype(BF16)
        dbc_ref[r * ROWS : (r + 1) * ROWS, :LANES] = dot(ds, c[r])
        dbc_ref[r * ROWS : (r + 1) * ROWS, LANES:] = dot(ds, b[r], TN)


def tap_sums(dpre, ext_ref):
    sums = [jnp.sum(dpre * ext_ref[pl.ds(HALO - 3 + k, SEG), :], 0, keepdims=True) for k in range(4)]
    return sums + [jnp.sum(dpre, 0, keepdims=True)]


def last_body(
    got_ref, halo_ref, rows_ref, cols_ref, bcact_ref, side_ref, states_ref,
    near_ref, dx_ref, slope_ref, xw_ref, gw_ref, dbc_ref, slope2_ref, row_ref,
    dpre_ref, gstep_ref, part_ref, ext_ref, ext2_ref, acc_ref,
):
    n = 2 * HEADS
    left = iota((ROWS, LANES), 1) < 64
    half = jnp.where((iota((8, LANES), 1) < 64) == (iota((8, LANES), 0) == 0), 1.0, 0.0).astype(BF16)
    b = [bcact_ref[r * ROWS : (r + 1) * ROWS, :LANES] for r in range(2)]
    c = [bcact_ref[r * ROWS : (r + 1) * ROWS, LANES:] for r in range(2)]
    db = [jnp.zeros((ROWS, LANES), F32) for _ in range(2)]
    dc = [jnp.zeros((ROWS, LANES), F32) for _ in range(2)]
    part_ref[...] = jnp.zeros(part_ref.shape, F32)
    pad = jnp.zeros((HALO, HALF + 2 * LANES), F32)
    dpre_ref[:HALO, :] = pad
    dpre_ref[HALO + SEG :, :] = pad
    for o in range(PAIRS):
        lanes = slice(o * LANES, (o + 1) * LANES)
        state, later = states_ref[o, :ROWS, :], states_ref[o, ROWS:, :]
        total = []
        for r in range(2):
            h = 3 * n + head_of(r, o)
            total.append(jnp.where(left[:1], cols_ref[ROWS - 1 :, h : h + 1], cols_ref[ROWS - 1 :, h + 1 : h + 2]))
        states = [state, (total[0] * state.astype(F32) + near_ref[o, :ROWS, :].astype(F32)).astype(BF16)]
        laters = [(total[1] * later.astype(F32) + near_ref[o, ROWS:, :].astype(F32)).astype(BF16), later]
        ext = ext_ref.at[o % 2]
        fill_pair(ext, got_ref, halo_ref, o)
        for r in range(2):
            rows = slice(r * ROWS, (r + 1) * ROWS)
            h = head_of(r, o)
            xw = xw_ref[o, rows]
            gw = gw_ref[o, rows]
            carried = dot(c[r], states[r]) * gw.astype(F32)
            dxw = dot(b[r], laters[r]).astype(BF16).astype(F32)
            dc[r] = dc[r] + dot(gw, states[r], NT)
            db[r] = db[r] + dot(xw, laters[r], NT)
            acc_ref[h : h + 2, :] = dot(half, carried.astype(BF16), NT)[:2]
            acc_ref[n + h : n + h + 2, :] = dot(half, (dxw * xw.astype(F32)).astype(BF16), NT)[:2]
            both = jnp.sum(states[r].astype(F32) * laters[r].astype(F32), 0, keepdims=True)
            acc_ref[2 * n + h : 2 * n + h + 1, :] = jnp.where(left[:1], both, 0.0)
            acc_ref[2 * n + h + 1 : 2 * n + h + 2, :] = jnp.where(left[:1], 0.0, both)
            dact = dx_ref[o, rows] + pair_column(cols_ref, 2, r, o, left) * dxw
            dpre_ref[HALO + r * ROWS : HALO + (r + 1) * ROWS, lanes] = dact.astype(BF16).astype(F32) * slope_ref[o, rows]
        sums = tap_sums(dpre_ref[HALO : HALO + SEG, lanes], ext)
        for k in range(5):
            part_ref[o, k : k + 1, :] = sums[k]
    fill_bc(ext2_ref, got_ref, halo_ref)
    dpre2 = jnp.concatenate([jnp.concatenate(db, 0), jnp.concatenate(dc, 0)], 1)
    dpre2 = (dbc_ref[...] + dpre2) * slope2_ref[...]
    dpre_ref[HALO : HALO + SEG, HALF:] = dpre2
    sums = tap_sums(dpre2, ext2_ref)
    for k in range(5):
        part_ref[k, 5:6, :] = sums[k][:, :LANES]
        part_ref[k, 6:7, :] = sums[k][:, LANES:]
    step = rows_ref[n : 2 * n, :]
    gate = rows_ref[4 * n : 5 * n, :]
    rate = rows_ref[5 * n : 6 * n, :]
    total = rows_ref[3 * n : 4 * n, ROWS - 1 :]
    at_t = row_ref[:n, :]
    at_s = row_ref[n : 2 * n, :]
    ended = acc_ref[n : 2 * n, :]
    at_end = jnp.sum(ended, 1, keepdims=True) + total * jnp.sum(acc_ref[2 * n :, :], 1, keepdims=True)
    final = iota((n, ROWS), 1) == ROWS - 1
    dcumul = at_t - at_s + acc_ref[:n, :] - ended + jnp.where(final, at_end, 0.0)
    onward = (iota((ROWS, ROWS), 0) >= iota((ROWS, ROWS), 1)).astype(F32)
    ddecay = dot(dcumul, onward, precision=HIGH)
    dstep = ((at_s + ended) / step + ddecay * rate) * gate
    gstep_ref[...] = dstep
    dbias = jnp.sum(dstep, 1, keepdims=True)
    drate = jnp.sum(ddecay * rate * step, 1, keepdims=True)
    dskip = jnp.sum(row_ref[2 * n :, :], 1, keepdims=True)
    second = jnp.broadcast_to(side_ref[:1] > 0.5, (n, LANES))
    at = iota((n, LANES), 1) - iota((n, LANES), 0) % HEADS - jnp.where(second, HEADS, 0)
    placed = jnp.where(at == 0, dbias, jnp.where(at == n, drate, jnp.where(at == 2 * n, dskip, 0.0)))
    part_ref[0, 7:8, :] = jnp.sum(placed, 0, keepdims=True)


def input_body(dpre_ref, taps_ref, gx_ref, gbc_ref, rim_ref):
    for o in range(PAIRS + 2):
        lanes = slice(o * LANES, (o + 1) * LANES)
        own = jnp.zeros((SEG, LANES), F32)
        rim = jnp.zeros((HALO, LANES), F32)
        for k in range(4):
            tap = taps_ref[k : k + 1, lanes]
            own = own + tap * dpre_ref[pl.ds(HALO + 3 - k, SEG), lanes]
            rim = rim + tap * dpre_ref[pl.ds(HALO - k, HALO), lanes]
        rim_ref[o, :, :] = rim.astype(BF16)
        if o < PAIRS:
            gx_ref[:, lanes] = own.astype(BF16)
        else:
            gbc_ref[:, (o - PAIRS) * LANES : (o - PAIRS + 1) * LANES] = own


def swap_body(gx_ref, gbc_ref, back_ref, gstep_ref, side_ref, keepx_ref, keepbc_ref, keepstep_ref, give_ref):
    second = side_ref[:1] > 0.5
    whole = jnp.broadcast_to(second, (ROWS, LANES))
    last = iota((HALO, LANES), 0) >= HALO - 3
    for o in range(PAIRS + 2):
        lanes = slice(o * LANES, (o + 1) * LANES)
        came = pltpu.roll(back_ref[o].astype(F32), HALO - 3, 0)
        came = jnp.where(last, came, 0.0)
        came = jnp.concatenate([jnp.zeros((ROWS - HALO, LANES), F32), came], 0)
        if o < PAIRS:
            first, then = gx_ref[:ROWS, lanes].astype(F32), gx_ref[ROWS:, lanes].astype(F32) + came
            keepx_ref[:, lanes] = jnp.where(whole, then, first).astype(BF16)
        else:
            mine = slice((o - PAIRS) * LANES, (o - PAIRS + 1) * LANES)
            first, then = gbc_ref[:ROWS, mine], gbc_ref[ROWS:, mine] + came
            keepbc_ref[:, mine] = jnp.where(whole, then, first)
        give_ref[o, :, :] = jnp.where(whole, first, then).astype(BF16)
    first, then = gstep_ref[:HEADS, :], gstep_ref[HEADS:, :]
    keepstep_ref[...] = jnp.where(whole[:HEADS], then, first)
    given = jnp.where(whole[:HEADS], first, then)
    high = given.astype(BF16)
    give_ref[PAIRS + 2, :HEADS, :] = high
    give_ref[PAIRS + 2, HEADS : 2 * HEADS, :] = (given - high.astype(F32)).astype(BF16)
    give_ref[PAIRS + 2, 2 * HEADS :, :] = jnp.zeros((ROWS - 2 * HEADS, LANES), BF16)


def merge_body(keepx_ref, keepbc_ref, keepstep_ref, came_ref, side_ref, gx_ref, gbc_ref, gstep_ref):
    second = side_ref[:1] > 0.5
    whole = jnp.broadcast_to(second, (ROWS, LANES))
    for o in range(PAIRS):
        lanes = slice(o * LANES, (o + 1) * LANES)
        mine, other = keepx_ref[:, lanes].astype(F32), came_ref[o].astype(F32)
        gx_ref[:, lanes] = jnp.where(whole, other, mine).astype(BF16)
        gx_ref[:, HALF + o * LANES : HALF + (o + 1) * LANES] = jnp.where(whole, mine, other).astype(BF16)
    for k in range(2):
        lanes = slice(k * LANES, (k + 1) * LANES)
        gbc_ref[:, lanes] = (keepbc_ref[:, lanes] + came_ref[PAIRS + k].astype(F32)).astype(BF16)
    mine = keepstep_ref[...]
    other = came_ref[PAIRS + 2, :HEADS, :].astype(F32) + came_ref[PAIRS + 2, HEADS : 2 * HEADS, :].astype(F32)
    gstep_ref[:HEADS, :] = jnp.where(whole[:HEADS], other, mine)
    gstep_ref[HEADS:, :] = jnp.where(whole[:HEADS], mine, other)


def spread_body(in_ref, out_ref, *, scale):
    total = in_ref[0]
    for j in range(1, in_ref.shape[0]):
        total = total + in_ref[j]
    total = total * scale
    for j in range(out_ref.shape[0]):
        out_ref[j] = total


def spread(x, count, scale):
    def body(in_ref, out_ref):
        spread_body(in_ref, out_ref, scale=scale)

    return call(body, [far(count, 8, LANES)], [VMEM])(x)[0]


def unpack_body(in_ref, weight_ref, offset_ref, bias_ref, rate_ref, skip_ref):
    heads = in_ref[0, 7:8, :] + in_ref[1, 7:8, :]
    for k, ref in enumerate((bias_ref, rate_ref, skip_ref)):
        ref[...] = heads[:, k * 2 * HEADS : (k + 1) * 2 * HEADS].reshape(2 * HEADS)
    for k in range(2):
        for o in range(PAIRS):
            lanes = slice(k * HALF + o * LANES, k * HALF + (o + 1) * LANES)
            weight_ref[:, lanes] = in_ref[2 * o + k, :4, :]
            offset_ref[lanes] = in_ref[2 * o + k, 4, :]
    for k in range(5):
        both = in_ref[2 * k, 5:7, :] + in_ref[2 * k + 1, 5:7, :]
        for m in range(2):
            lanes = slice(2 * HALF + m * LANES, 2 * HALF + (m + 1) * LANES)
            if k < 4:
                weight_ref[k : k + 1, lanes] = both[m : m + 1]
            else:
                offset_ref[lanes] = both[m]


def compute(
    mixer_input, state_input, step_raw, conv_weight, conv_bias, step_bias, log_rate, skip_gain, grad_out
):
    x, bc, step, g = mixer_input[0], state_input[0], step_raw[0], grad_out[0]
    n_seq, n_dp = lax.axis_size("seq"), lax.axis_size("dp")
    chips = n_seq // 2
    inner = 2 * HALF
    n = 2 * HEADS
    assert x.shape == (ROWS, inner) and bc.shape == (ROWS, 2 * LANES) and chips == PAIRS and step.shape[0] == n
    cores = [[2 * c, 2 * c + 1] for c in range(chips)]
    ring = [[2 * c + k for c in range(chips)] for k in range(2)]
    packed = call(pack_body, [shape(2, PACKED, LANES, dtype=BF16)], [FAR] * 4)(x, bc, g, step)[0]
    got = lax.all_to_all(packed, "seq", 0, 0, axis_index_groups=cores)
    tail = call(tail_body, [kept(PAIRS + 2, HALO, LANES, dtype=BF16)], [VMEM])(got)[0]
    halo = lax.ppermute(tail, "seq", [(i, i + 2) for i in range(n_seq - 2)])
    by_row, by_col, taps, side = call(
        steps_body,
        [kept(7 * n, ROWS), kept(ROWS, 4 * n), kept(5, HALF + 2 * LANES), kept(8, LANES)],
        [VMEM, FAR, FAR, SMEM, SMEM, SMEM],
    )(got, conv_weight, conv_bias, step_bias, log_rate, skip_gain)
    ext = [pltpu.VMEM((2, SEG + HALO, LANES), F32), pltpu.VMEM((SEG + HALO, 2 * LANES), F32)]
    bc_act, near, send = call(
        first_body,
        [
            kept(SEG, 2 * LANES, dtype=BF16),
            far(PAIRS, 2 * ROWS, LANES, dtype=BF16),
            shape(PAIRS, SENT, LANES, dtype=BF16),
        ],
        [VMEM] * 4,
        ext,
    )(got, halo, taps, by_col)
    sent = lax.all_to_all(send, "seq", 0, 0, axis_index_groups=ring)
    dx, slope, xw, gw, dbc, slope2, row = call(
        inner_body,
        [
            far(PAIRS, SEG, LANES),
            far(PAIRS, SEG, LANES),
            far(PAIRS, SEG, LANES, dtype=BF16),
            far(PAIRS, SEG, LANES, dtype=BF16),
            far(SEG, 2 * LANES),
            far(SEG, 2 * LANES),
            far(3 * n, ROWS),
        ],
        [VMEM] * 6,
        ext,
    )(got, halo, taps, by_row, by_col, bc_act)
    scanned = call(scan_body, [far(chips, 2 * ROWS, LANES, dtype=BF16)], [VMEM])(sent)[0]
    states = lax.all_to_all(scanned, "seq", 0, 0, axis_index_groups=ring)
    dpre, gstep, part = call(
        last_body,
        [kept(SEG + 2 * HALO, HALF + 2 * LANES), far(n, ROWS), far(PAIRS, 8, LANES)],
        [VMEM] * 7 + [FAR] * 8,
        ext + [pltpu.VMEM((3 * n, ROWS), F32)],
    )(got, halo, by_row, by_col, bc_act, side, states, near, dx, slope, xw, gw, dbc, slope2, row)
    part = lax.all_to_all(part, "seq", 0, 0, axis_index_groups=ring)
    part = spread(part, n_dp, 1.0)
    part = lax.all_to_all(part, "dp", 0, 0)
    part = spread(part, n_seq, 1.0 / n_dp)
    part = lax.all_to_all(part, "seq", 0, 0)
    gx, gbc, rim = call(
        input_body,
        [kept(SEG, HALF, dtype=BF16), kept(SEG, 2 * LANES), kept(PAIRS + 2, HALO, LANES, dtype=BF16)],
        [VMEM] * 2,
    )(dpre, taps)
    back = lax.ppermute(rim, "seq", [(i, i - 2) for i in range(2, n_seq)])
    keepx, keepbc, keepstep, give = call(
        swap_body,
        [
            kept(ROWS, HALF, dtype=BF16),
            kept(ROWS, 2 * LANES),
            kept(HEADS, ROWS),
            kept(PAIRS + 3, ROWS, LANES, dtype=BF16),
        ],
        [VMEM, VMEM, VMEM, FAR, VMEM],
    )(gx, gbc, back, gstep, side)
    came = lax.ppermute(give, "seq", [(i, i ^ 1) for i in range(n_seq)])
    gx, gbc, gstep = call(
        merge_body, [shape(ROWS, inner, dtype=BF16), shape(ROWS, 2 * LANES, dtype=BF16), shape(n, ROWS)], [VMEM] * 5
    )(keepx, keepbc, keepstep, came, side)
    weight, offset, bias, rate, skip = call(
        unpack_body,
        [shape(4, inner + 2 * LANES), shape(inner + 2 * LANES), shape(n), shape(n), shape(n)],
        [VMEM],
    )(part)
    return gx[None], gbc[None], gstep[None], weight, offset, bias, rate, skip


def solution(mesh):
    return jax.shard_map(
        compute,
        mesh=mesh,
        in_specs=(
            P("dp", "seq", None),
            P("dp", "seq", None),
            P("dp", None, "seq"),
            P(),
            P(),
            P(),
            P(),
            P(),
            P("dp", "seq", None),
        ),
        out_specs=(
            P("dp", "seq", None),
            P("dp", "seq", None),
            P("dp", None, "seq"),
            P(),
            P(),
            P(),
            P(),
            P(),
        ),
        check_vma=False,
    )
```

```python
import jax
import jax.numpy as jnp
from jax import lax
from jax.experimental import pallas as pl
from jax.experimental.pallas import tpu as pltpu
from jax.sharding import PartitionSpec as P


HIGH = lax.Precision.HIGHEST
F32 = jnp.float32
BF16 = jnp.bfloat16
ROWS = 128
LANES = 128
HALO = 8
PAIRS = 8
HEADS = 16
HALF = PAIRS * LANES
WIDE = 2 * LANES
SEG = 2 * ROWS
G_AT, B_AT, C_AT, STEP_AT = HALF, 2 * HALF, 2 * HALF + ROWS, 2 * HALF + 2 * ROWS
SIDE_AT = STEP_AT + 3 * HEADS
PACKED = SIDE_AT + 16
SENT = 2 * ROWS + 8
VMEM = pl.BlockSpec(memory_space=pltpu.VMEM)
FAR = pl.BlockSpec(memory_space=pltpu.VMEM)
SMEM = pl.BlockSpec(memory_space=pltpu.SMEM)
INTERPRET = False
NT = ((1,), (1,))
TN = ((0,), (0,))


def call(body, outs, ins, scratch=()):
    kernel = pl.pallas_call(
        body,
        out_shape=outs,
        in_specs=ins,
        out_specs=[VMEM] * len(outs),
        scratch_shapes=list(scratch),
        compiler_params=pltpu.CompilerParams(vmem_limit_bytes=16 << 20),
        interpret=INTERPRET,
    )
    if INTERPRET:
        return kernel
    return lambda *given: kernel(
        *(
            pltpu.with_memory_space_constraint(a, pltpu.VMEM if spec is VMEM else pltpu.HBM)
            for a, spec in zip(given, ins, strict=True)
        )
    )


def shape(*dims, dtype=F32):
    return jax.ShapeDtypeStruct(dims, dtype)


def far(*dims, dtype=F32):
    return shape(*dims, dtype=dtype) if INTERPRET else pltpu.HBM(dims, dtype)


def kept(*dims, dtype=F32):
    return shape(*dims, dtype=dtype) if INTERPRET else pltpu.VMEM(dims, dtype)


def dot(a, b, dims=((1,), (0,)), precision=None):
    return lax.dot_general(a, b, (dims, ((), ())), precision=precision, preferred_element_type=F32)


def iota(dims, axis):
    return lax.broadcasted_iota(jnp.int32, dims, axis)


def pack_body(x_ref, bc_ref, g_ref, step_ref, out_ref):
    bc = bc_ref[...]
    for q in range(2):
        for o in range(PAIRS):
            at = q * HALF + o * LANES
            out_ref[q, o * ROWS : (o + 1) * ROWS, :] = x_ref[:, at : at + LANES]
            out_ref[q, G_AT + o * ROWS : G_AT + (o + 1) * ROWS, :] = g_ref[:, at : at + LANES]
        out_ref[q, B_AT : B_AT + ROWS, :] = bc[:, :LANES]
        out_ref[q, C_AT : C_AT + ROWS, :] = bc[:, LANES:]
        rest = step_ref[q * HEADS : (q + 1) * HEADS, :]
        for k in range(3):
            piece = rest.astype(BF16)
            rest = rest - piece.astype(F32)
            out_ref[q, STEP_AT + k * HEADS : STEP_AT + (k + 1) * HEADS, :] = piece
        out_ref[q, SIDE_AT:, :] = jnp.full((16, LANES), float(q), F32).astype(BF16)


def tail_body(got_ref, out_ref):
    for o in range(PAIRS):
        out_ref[o, :, :] = got_ref[1, (o + 1) * ROWS - HALO : (o + 1) * ROWS, :]
    out_ref[PAIRS, :, :] = got_ref[1, B_AT + ROWS - HALO : B_AT + ROWS, :]
    out_ref[PAIRS + 1, :, :] = got_ref[1, C_AT + ROWS - HALO : C_AT + ROWS, :]


def head_rows(ref, second):
    rows = iota((2 * HEADS, LANES), 0) % HEADS
    out = jnp.zeros((2 * HEADS, LANES), F32)
    for h in range(HEADS):
        out = jnp.where(rows == h, jnp.where(second, ref[HEADS + h], ref[h]), out)
    return out


def steps_body(got_ref, weight_ref, offset_ref, bias_ref, rate_ref, skip_ref, rows_ref, cols_ref, taps_ref, side_ref, parts_ref):
    side = got_ref[0, SIDE_AT:, :].astype(F32)[:8]
    side_ref[...] = side
    second = side[:1] > 0.5
    offset = offset_ref[...].reshape(1, -1)
    inner = 2 * HALF
    for o in range(PAIRS):
        at = o * LANES
        lanes = slice(at, at + LANES)
        other = slice(HALF + at, HALF + at + LANES)
        taps_ref[:4, lanes] = jnp.where(second, weight_ref[:, other], weight_ref[:, lanes])
        taps_ref[4:5, lanes] = jnp.where(second, offset[:, other], offset[:, lanes])
    taps_ref[:4, HALF:] = weight_ref[:, inner:]
    taps_ref[4:5, HALF:] = offset[:, inner:]
    n = 2 * HEADS
    raw = [
        sum(got_ref[r, STEP_AT + k * HEADS : STEP_AT + (k + 1) * HEADS, :].astype(F32) for k in (2, 1, 0)) for r in range(2)
    ]
    second = jnp.broadcast_to(second, (n, LANES))
    raw = jnp.concatenate(raw, 0) + head_rows(bias_ref, second)
    step = jnp.maximum(raw, 0.0) + jnp.log1p(jnp.exp(-jnp.abs(raw)))
    rate = -jnp.exp(head_rows(rate_ref, second))
    upto = (iota((ROWS, ROWS), 0) <= iota((ROWS, ROWS), 1)).astype(F32)
    cumul = dot(rate * step, upto, precision=HIGH)
    weight = jnp.exp(cumul[:, ROWS - 1 :] - cumul) * step
    fade = jnp.exp(cumul)
    stack = jnp.concatenate([cumul, step, weight, fade], 0)
    rows_ref[: 4 * n, :] = stack
    rows_ref[4 * n : 5 * n, :] = jax.nn.sigmoid(raw)
    rows_ref[5 * n : 6 * n, :] = rate
    rows_ref[6 * n :, :] = head_rows(skip_ref, second)
    cols_ref[...] = stack.T
    for k, value in enumerate((weight, fade)):
        split = [value]
        for _ in range(2):
            split.append(split[-1] - split[-1].astype(BF16).astype(F32))
        for r in range(2):
            for c in range(HALF // WIDE):
                at = r * HEADS + 4 * c
                rows = [piece[at : at + 4] for piece in split] + [jnp.zeros((4, ROWS), F32)]
                parts_ref[k, r, c] = jnp.concatenate(rows, 0).astype(BF16)


def spreader():
    part, head = iota((16, WIDE), 0), iota((16, WIDE), 1) // 64
    return jnp.where((part % 4 == head) & (part < 12), 1.0, 0.0).astype(BF16)


def beside(first, second):
    return jnp.concatenate([first, second], 1)


def head_of(r, o):
    return r * HEADS + 2 * o


def fill(ext_ref, got_ref, halo_ref):
    for o in range(PAIRS + 2):
        at = o * ROWS if o < PAIRS else B_AT + (o - PAIRS) * ROWS
        ext_ref[o, :HALO, :] = halo_ref[o].astype(F32)
        for r in range(2):
            ext_ref[o, HALO + r * ROWS : HALO + (r + 1) * ROWS, :] = got_ref[r, at : at + ROWS, :].astype(F32)


def preact(ext_ref, taps_ref, o, first=0, count=SEG):
    lanes = slice(o * LANES, (o + 1) * LANES)
    acc = taps_ref[4:5, lanes]
    for k in range(4):
        acc = acc + taps_ref[k : k + 1, lanes] * ext_ref[o, pl.ds(HALO - 3 + k + first, count), :]
    return acc


def pair_column(cols_ref, which, r, o, left):
    at = which * 2 * HEADS + head_of(r, o)
    a = jnp.broadcast_to(cols_ref[:, at : at + 1], (ROWS, LANES))
    b = jnp.broadcast_to(cols_ref[:, at + 1 : at + 2], (ROWS, LANES))
    return jnp.where(left, a, b)


def decay_of(tail):
    tail = tail.astype(F32)
    return tail[0:1, :] + tail[1:2, :]


def decay_rows(total):
    high = total.astype(BF16).astype(F32)
    row = iota((8, LANES), 0)
    return jnp.where(row == 0, high, jnp.where(row == 1, total - high, 0.0)).astype(BF16)


def first_body(got_ref, halo_ref, taps_ref, parts_ref, bcact_ref, near_ref, send_ref, ext_ref):
    fill(ext_ref, got_ref, halo_ref)
    pre = beside(preact(ext_ref, taps_ref, PAIRS), preact(ext_ref, taps_ref, PAIRS + 1))
    bc = pre * jax.nn.sigmoid(pre)
    bcact_ref[...] = bc.astype(BF16)
    bc = bc.astype(BF16).astype(F32)
    b_t = [bc[r * ROWS : (r + 1) * ROWS, :LANES].T.astype(BF16) for r in range(2)]
    c_t = [bc[r * ROWS : (r + 1) * ROWS, LANES:].T.astype(BF16) for r in range(2)]
    over = spreader()
    for c in range(HALF // WIDE):
        ends, backs, totals = [], [], []
        g_at = G_AT + 2 * c * ROWS
        for r in range(2):
            pre = beside(*(preact(ext_ref, taps_ref, 2 * c + k, r * ROWS, ROWS) for k in range(2)))
            act = (pre * jax.nn.sigmoid(pre)).astype(BF16).astype(F32)
            fade = dot(parts_ref[1, r, c], over, TN)
            xw = (act * dot(parts_ref[0, r, c], over, TN)).astype(BF16)
            g = beside(got_ref[r, g_at : g_at + ROWS, :], got_ref[r, g_at + ROWS : g_at + 2 * ROWS, :])
            gw = (g.astype(F32) * fade).astype(BF16)
            ends.append(dot(b_t[r], xw))
            backs.append(dot(c_t[r], gw))
            totals.append(fade[ROWS - 1 :, :])
        end = totals[1] * ends[0] + ends[1]
        back = backs[0] + totals[0] * backs[1]
        total = totals[0] * totals[1]
        for k in range(2):
            o, lanes = 2 * c + k, slice(k * LANES, (k + 1) * LANES)
            near_ref[o, :ROWS, :] = ends[0][:, lanes].astype(BF16)
            near_ref[o, ROWS:, :] = backs[1][:, lanes].astype(BF16)
            send_ref[o, :ROWS, :] = end[:, lanes].astype(BF16)
            send_ref[o, ROWS : 2 * ROWS, :] = back[:, lanes].astype(BF16)
            send_ref[o, 2 * ROWS :, :] = decay_rows(total[:, lanes])


def scan_body(got_ref, out_ref):
    count = got_ref.shape[0]
    state = jnp.zeros((ROWS, LANES), F32)
    for j in range(count):
        out_ref[j, :ROWS, :] = state.astype(BF16)
        state = decay_of(got_ref[j, 2 * ROWS :, :]) * state + got_ref[j, :ROWS, :].astype(F32)
    state = jnp.zeros((ROWS, LANES), F32)
    for j in range(count - 1, -1, -1):
        out_ref[j, ROWS:, :] = state.astype(BF16)
        state = decay_of(got_ref[j, 2 * ROWS :, :]) * state + got_ref[j, ROWS : 2 * ROWS, :].astype(F32)


def inner_body(
    got_ref, halo_ref, taps_ref, rows_ref, cols_ref, bcact_ref,
    dx_ref, slope_ref, xw_ref, gw_ref, dbc_ref, slope2_ref, row_ref, ext_ref,
):
    n = 2 * HEADS
    fill(ext_ref, got_ref, halo_ref)
    pre = beside(preact(ext_ref, taps_ref, PAIRS), preact(ext_ref, taps_ref, PAIRS + 1))
    gate = jax.nn.sigmoid(pre)
    slope2_ref[...] = gate * (1.0 + pre * (1.0 - gate))
    causal = iota((ROWS, ROWS), 0) <= iota((ROWS, ROWS), 1)
    left = iota((ROWS, LANES), 1) < 64
    ones = jnp.ones((8, ROWS), BF16)
    b = [bcact_ref[r * ROWS : (r + 1) * ROWS, :LANES] for r in range(2)]
    c = [bcact_ref[r * ROWS : (r + 1) * ROWS, LANES:] for r in range(2)]
    scores = [dot(b[r], c[r], NT) for r in range(2)]
    dscores = [jnp.zeros((ROWS, ROWS), F32) for _ in range(2)]
    for o in range(PAIRS):
        lanes = slice(o * LANES, (o + 1) * LANES)
        pre = preact(ext_ref, taps_ref, o)
        gate = jax.nn.sigmoid(pre)
        slope_ref[:, lanes] = (gate * (1.0 + pre * (1.0 - gate))).astype(BF16)
        whole = (pre * gate).astype(BF16)
        for r in range(2):
            h = head_of(r, o)
            rows = slice(r * ROWS, (r + 1) * ROWS)
            act = whole[rows]
            wide = got_ref[r, G_AT + o * ROWS : G_AT + (o + 1) * ROWS, :].astype(F32)
            xw_ref[rows, lanes] = (act.astype(F32) * pair_column(cols_ref, 2, r, o, left)).astype(BF16)
            gw_ref[rows, lanes] = (wide * pair_column(cols_ref, 3, r, o, left)).astype(BF16)
            skip = jnp.where(left[:1], rows_ref[6 * n + h : 6 * n + h + 1, :], rows_ref[6 * n + h + 1 : 6 * n + h + 2, :])
            dx = skip * wide
            both = jnp.sum(act.astype(F32) * wide, 0, keepdims=True)
            row_ref[2 * n + h : 2 * n + h + 1, :] = jnp.where(left[:1], both, 0.0)
            row_ref[2 * n + h + 1 : 2 * n + h + 2, :] = jnp.where(left[:1], 0.0, both)
            for k in range(2):
                own = jnp.where(left if k == 0 else ~left, wide, 0.0).astype(BF16)
                gap = rows_ref[h + k : h + k + 1, :] - cols_ref[:, h + k : h + k + 1]
                fall = jnp.exp(jnp.where(causal, gap, -1e30)) * cols_ref[:, n + h + k : n + h + k + 1]
                mixing = scores[r] * fall
                dmix = dot(act, own, NT).astype(BF16).astype(F32)
                dscores[r] = dscores[r] + dmix * fall
                both = (dmix * mixing).astype(BF16)
                row_ref[h + k : h + k + 1, :] = dot(ones, both)[:1]
                row_ref[n + h + k : n + h + k + 1, :] = dot(ones, both, NT)[:1]
                dx = dx + dot(mixing.astype(BF16), own)
            dx_ref[rows, lanes] = dx.astype(BF16)
    for r in range(2):
        ds = dscores[r].astype(BF16)
        dbc_ref[r * ROWS : (r + 1) * ROWS, :LANES] = dot(ds, c[r])
        dbc_ref[r * ROWS : (r + 1) * ROWS, LANES:] = dot(ds, b[r], TN)


def tap_sums(dpre_ref, ext_ref, o):
    dpre = dpre_ref[o, HALO : HALO + SEG, :]
    sums = [jnp.sum(dpre * ext_ref[o, pl.ds(HALO - 3 + k, SEG), :], 0, keepdims=True) for k in range(4)]
    return sums + [jnp.sum(dpre, 0, keepdims=True)]


def last_body(
    got_ref, halo_ref, rows_ref, cols_ref, parts_ref, bcact_ref, side_ref, states_ref,
    near_ref, dx_ref, slope_ref, xw_ref, gw_ref, dbc_ref, slope2_ref, row_ref,
    dpre_ref, gstep_ref, part_ref, ext_ref, acc_ref, state_ref, later_ref, sums_ref,
):
    n = 2 * HEADS
    left = iota((1, LANES), 1) < 64
    quarter = iota((1, WIDE), 1) // 64
    b = [bcact_ref[r * ROWS : (r + 1) * ROWS, :LANES] for r in range(2)]
    c = [bcact_ref[r * ROWS : (r + 1) * ROWS, LANES:] for r in range(2)]
    fill(ext_ref, got_ref, halo_ref)
    part_ref[...] = jnp.zeros(part_ref.shape, F32)
    pad = jnp.zeros((PAIRS + 2, HALO, LANES), F32)
    dpre_ref[:, :HALO, :] = pad
    dpre_ref[:, HALO + SEG :, :] = pad
    over = spreader()
    for m in range(HALF // WIDE):
        lanes = slice(m * WIDE, (m + 1) * WIDE)
        total = []
        for r in range(2):
            h = 3 * n + r * HEADS + 4 * m
            row = cols_ref[ROWS - 1 :, h : h + 1]
            for k in range(1, 4):
                row = jnp.where(quarter >= k, cols_ref[ROWS - 1 :, h + k : h + k + 1], row)
            total.append(row)
        state, later, near, near_later = (
            beside(ref[2 * m, rows, :], ref[2 * m + 1, rows, :])
            for ref in (states_ref, near_ref)
            for rows in (slice(0, ROWS), slice(ROWS, 2 * ROWS))
        )
        states = [state, (total[0] * state.astype(F32) + near.astype(F32)).astype(BF16)]
        laters = [(total[1] * later.astype(F32) + near_later.astype(F32)).astype(BF16), later]
        for r in range(2):
            rows = slice(r * ROWS, (r + 1) * ROWS)
            state_ref[r, :, lanes] = states[r]
            later_ref[r, :, lanes] = laters[r]
            xw = xw_ref[rows, lanes].astype(F32)
            sums_ref[rows, lanes] = (dot(c[r], states[r]) * gw_ref[rows, lanes].astype(F32)).astype(BF16)
            dxw = dot(b[r], laters[r])
            sums_ref[rows, HALF + m * WIDE : HALF + (m + 1) * WIDE] = (dxw * xw).astype(BF16)
            both = jnp.sum(states[r].astype(F32) * laters[r].astype(F32), 0, keepdims=True)
            for k in range(2):
                h = head_of(r, 2 * m + k)
                mine = both[:, k * LANES : (k + 1) * LANES]
                acc_ref[h : h + 1, :] = jnp.where(left, mine, 0.0)
                acc_ref[h + 1 : h + 2, :] = jnp.where(left, 0.0, mine)
            dact = dx_ref[rows, lanes].astype(F32) + dot(parts_ref[0, r, m], over, TN) * dxw
            dact = dact * slope_ref[rows, lanes].astype(F32)
            for k in range(2):
                dpre_ref[2 * m + k, HALO + r * ROWS : HALO + (r + 1) * ROWS, :] = dact[:, k * LANES : (k + 1) * LANES]
    dpre2 = []
    for r in range(2):
        rows = slice(r * ROWS, (r + 1) * ROWS)
        dpre2.append(beside(dot(xw_ref[rows, :], later_ref[r], NT), dot(gw_ref[rows, :], state_ref[r], NT)))
    dpre2 = (dbc_ref[...] + jnp.concatenate(dpre2, 0)) * slope2_ref[...]
    for k in range(2):
        dpre_ref[PAIRS + k, HALO : HALO + SEG, :] = dpre2[:, k * LANES : (k + 1) * LANES]
    for o in range(PAIRS + 2):
        sums = tap_sums(dpre_ref, ext_ref, o)
        for k in range(5):
            if o < PAIRS:
                part_ref[o, k : k + 1, :] = sums[k]
            else:
                part_ref[k, 5 + o - PAIRS : 6 + o - PAIRS, :] = sums[k]
    lane = iota((16, LANES), 1)
    pick = [jnp.where(lane == h, 1.0, 0.0).astype(BF16) for h in range(n)]
    pick = jnp.concatenate([p for p in pick for _ in range(4)], 0)
    by_head = dot(sums_ref[...], pick)
    by_head = [by_head[r * ROWS : (r + 1) * ROWS].T for r in range(2)]
    entered = jnp.concatenate([t[:HEADS] for t in by_head], 0)
    ended = jnp.concatenate([t[HEADS:n] for t in by_head], 0)
    step = rows_ref[n : 2 * n, :]
    gate = rows_ref[4 * n : 5 * n, :]
    rate = rows_ref[5 * n : 6 * n, :]
    total = rows_ref[3 * n : 4 * n, ROWS - 1 :]
    at_t = row_ref[:n, :]
    at_s = row_ref[n : 2 * n, :]
    at_end = jnp.sum(ended, 1, keepdims=True) + total * jnp.sum(acc_ref[...], 1, keepdims=True)
    final = iota((n, ROWS), 1) == ROWS - 1
    dcumul = at_t - at_s + entered - ended + jnp.where(final, at_end, 0.0)
    onward = (iota((ROWS, ROWS), 0) >= iota((ROWS, ROWS), 1)).astype(F32)
    ddecay = dot(dcumul, onward, precision=HIGH)
    dstep = ((at_s + ended) / step + ddecay * rate) * gate
    gstep_ref[...] = dstep
    dbias = jnp.sum(dstep, 1, keepdims=True)
    drate = jnp.sum(ddecay * rate * step, 1, keepdims=True)
    dskip = jnp.sum(row_ref[2 * n :, :], 1, keepdims=True)
    second = jnp.broadcast_to(side_ref[:1] > 0.5, (n, LANES))
    at = iota((n, LANES), 1) - iota((n, LANES), 0) % HEADS - jnp.where(second, HEADS, 0)
    placed = jnp.where(at == 0, dbias, jnp.where(at == n, drate, jnp.where(at == 2 * n, dskip, 0.0)))
    part_ref[0, 7:8, :] = jnp.sum(placed, 0, keepdims=True)


def input_body(dpre_ref, taps_ref, gx_ref, gbc_ref, rim_ref):
    for o in range(PAIRS + 2):
        lanes = slice(o * LANES, (o + 1) * LANES)
        own = jnp.zeros((SEG, LANES), F32)
        rim = jnp.zeros((HALO, LANES), F32)
        for k in range(4):
            tap = taps_ref[k : k + 1, lanes]
            own = own + tap * dpre_ref[o, pl.ds(HALO + 3 - k, SEG), :]
            rim = rim + tap * dpre_ref[o, pl.ds(HALO - k, HALO), :]
        rim_ref[o, :, :] = rim.astype(BF16)
        if o < PAIRS:
            gx_ref[:, lanes] = own.astype(BF16)
        else:
            gbc_ref[:, (o - PAIRS) * LANES : (o - PAIRS + 1) * LANES] = own


def swap_body(gx_ref, gbc_ref, back_ref, gstep_ref, side_ref, keepx_ref, keepbc_ref, keepstep_ref, give_ref):
    second = side_ref[:1] > 0.5
    whole = jnp.broadcast_to(second, (ROWS, LANES))
    last = iota((HALO, LANES), 0) >= HALO - 3
    for o in range(PAIRS + 2):
        lanes = slice(o * LANES, (o + 1) * LANES)
        came = pltpu.roll(back_ref[o].astype(F32), HALO - 3, 0)
        came = jnp.where(last, came, 0.0)
        came = jnp.concatenate([jnp.zeros((ROWS - HALO, LANES), F32), came], 0)
        if o < PAIRS:
            first, then = gx_ref[:ROWS, lanes].astype(F32), gx_ref[ROWS:, lanes].astype(F32) + came
            keepx_ref[:, lanes] = jnp.where(whole, then, first).astype(BF16)
        else:
            mine = slice((o - PAIRS) * LANES, (o - PAIRS + 1) * LANES)
            first, then = gbc_ref[:ROWS, mine], gbc_ref[ROWS:, mine] + came
            keepbc_ref[:, mine] = jnp.where(whole, then, first)
        give_ref[o, :, :] = jnp.where(whole, first, then).astype(BF16)
    first, then = gstep_ref[:HEADS, :], gstep_ref[HEADS:, :]
    keepstep_ref[...] = jnp.where(whole[:HEADS], then, first)
    given = jnp.where(whole[:HEADS], first, then)
    high = given.astype(BF16)
    give_ref[PAIRS + 2, :HEADS, :] = high
    give_ref[PAIRS + 2, HEADS : 2 * HEADS, :] = (given - high.astype(F32)).astype(BF16)
    give_ref[PAIRS + 2, 2 * HEADS :, :] = jnp.zeros((ROWS - 2 * HEADS, LANES), BF16)


def merge_body(keepx_ref, keepbc_ref, keepstep_ref, came_ref, side_ref, gx_ref, gbc_ref, gstep_ref):
    second = side_ref[:1] > 0.5
    whole = jnp.broadcast_to(second, (ROWS, LANES))
    for o in range(PAIRS):
        lanes = slice(o * LANES, (o + 1) * LANES)
        mine, other = keepx_ref[:, lanes].astype(F32), came_ref[o].astype(F32)
        gx_ref[:, lanes] = jnp.where(whole, other, mine).astype(BF16)
        gx_ref[:, HALF + o * LANES : HALF + (o + 1) * LANES] = jnp.where(whole, mine, other).astype(BF16)
    for k in range(2):
        lanes = slice(k * LANES, (k + 1) * LANES)
        gbc_ref[:, lanes] = (keepbc_ref[:, lanes] + came_ref[PAIRS + k].astype(F32)).astype(BF16)
    mine = keepstep_ref[...]
    other = came_ref[PAIRS + 2, :HEADS, :].astype(F32) + came_ref[PAIRS + 2, HEADS : 2 * HEADS, :].astype(F32)
    gstep_ref[:HEADS, :] = jnp.where(whole[:HEADS], other, mine)
    gstep_ref[HEADS:, :] = jnp.where(whole[:HEADS], mine, other)


def spread_body(in_ref, out_ref, *, scale):
    total = in_ref[0]
    for j in range(1, in_ref.shape[0]):
        total = total + in_ref[j]
    total = total * scale
    for j in range(out_ref.shape[0]):
        out_ref[j] = total


def spread(x, count, scale):
    def body(in_ref, out_ref):
        spread_body(in_ref, out_ref, scale=scale)

    return call(body, [far(count, 8, LANES)], [VMEM])(x)[0]


def unpack_body(in_ref, weight_ref, offset_ref, bias_ref, rate_ref, skip_ref):
    heads = in_ref[0, 7:8, :] + in_ref[1, 7:8, :]
    for k, ref in enumerate((bias_ref, rate_ref, skip_ref)):
        ref[...] = heads[:, k * 2 * HEADS : (k + 1) * 2 * HEADS].reshape(2 * HEADS)
    for k in range(2):
        for o in range(PAIRS):
            lanes = slice(k * HALF + o * LANES, k * HALF + (o + 1) * LANES)
            weight_ref[:, lanes] = in_ref[2 * o + k, :4, :]
            offset_ref[lanes] = in_ref[2 * o + k, 4, :]
    for k in range(5):
        both = in_ref[2 * k, 5:7, :] + in_ref[2 * k + 1, 5:7, :]
        for m in range(2):
            lanes = slice(2 * HALF + m * LANES, 2 * HALF + (m + 1) * LANES)
            if k < 4:
                weight_ref[k : k + 1, lanes] = both[m : m + 1]
            else:
                offset_ref[lanes] = both[m]


def compute(
    mixer_input, state_input, step_raw, conv_weight, conv_bias, step_bias, log_rate, skip_gain, grad_out
):
    x, bc, step, g = mixer_input[0], state_input[0], step_raw[0], grad_out[0]
    n_seq, n_dp = lax.axis_size("seq"), lax.axis_size("dp")
    chips = n_seq // 2
    inner = 2 * HALF
    n = 2 * HEADS
    assert x.shape == (ROWS, inner) and bc.shape == (ROWS, 2 * LANES) and chips == PAIRS and step.shape[0] == n
    cores = [[2 * c, 2 * c + 1] for c in range(chips)]
    ring = [[2 * c + k for c in range(chips)] for k in range(2)]
    packed = call(pack_body, [shape(2, PACKED, LANES, dtype=BF16)], [FAR] * 4)(x, bc, g, step)[0]
    got = lax.all_to_all(packed, "seq", 0, 0, axis_index_groups=cores)
    tail = call(tail_body, [kept(PAIRS + 2, HALO, LANES, dtype=BF16)], [VMEM])(got)[0]
    halo = lax.ppermute(tail, "seq", [(i, i + 2) for i in range(n_seq - 2)])
    by_row, by_col, taps, side, parts = call(
        steps_body,
        [
            kept(7 * n, ROWS),
            kept(ROWS, 4 * n),
            kept(5, HALF + 2 * LANES),
            kept(8, LANES),
            kept(2, 2, HALF // WIDE, 16, ROWS, dtype=BF16),
        ],
        [VMEM, FAR, FAR, SMEM, SMEM, SMEM],
    )(got, conv_weight, conv_bias, step_bias, log_rate, skip_gain)
    ext = [pltpu.VMEM((PAIRS + 2, SEG + HALO, LANES), F32)]
    bc_act, near, send = call(
        first_body,
        [
            kept(SEG, 2 * LANES, dtype=BF16),
            kept(PAIRS, 2 * ROWS, LANES, dtype=BF16),
            far(PAIRS, SENT, LANES, dtype=BF16),
        ],
        [VMEM] * 4,
        ext,
    )(got, halo, taps, parts)
    sent = lax.all_to_all(send, "seq", 0, 0, axis_index_groups=ring)
    dx, slope, xw, gw, dbc, slope2, row = call(
        inner_body,
        [
            far(SEG, HALF, dtype=BF16),
            far(SEG, HALF, dtype=BF16),
            far(SEG, HALF, dtype=BF16),
            far(SEG, HALF, dtype=BF16),
            far(SEG, 2 * LANES),
            far(SEG, 2 * LANES),
            far(3 * n, ROWS),
        ],
        [VMEM] * 6,
        ext,
    )(got, halo, taps, by_row, by_col, bc_act)
    scanned = call(scan_body, [shape(chips, 2 * ROWS, LANES, dtype=BF16)], [VMEM])(sent)[0]
    states = lax.all_to_all(scanned, "seq", 0, 0, axis_index_groups=ring)
    dpre, gstep, part = call(
        last_body,
        [kept(PAIRS + 2, SEG + 2 * HALO, LANES), far(n, ROWS), far(PAIRS, 8, LANES)],
        [VMEM] * 13 + [FAR] * 3,
        ext
        + [
            pltpu.VMEM((n, ROWS), F32),
            pltpu.VMEM((2, ROWS, HALF), BF16),
            pltpu.VMEM((2, ROWS, HALF), BF16),
            pltpu.VMEM((SEG, 2 * HALF), BF16),
        ],
    )(got, halo, by_row, by_col, parts, bc_act, side, states, near, dx, slope, xw, gw, dbc, slope2, row)
    part = lax.all_to_all(part, "seq", 0, 0, axis_index_groups=ring)
    part = spread(part, n_dp, 1.0)
    part = lax.all_to_all(part, "dp", 0, 0)
    part = spread(part, n_seq, 1.0 / n_dp)
    part = lax.all_to_all(part, "seq", 0, 0)
    gx, gbc, rim = call(
        input_body,
        [kept(SEG, HALF, dtype=BF16), kept(SEG, 2 * LANES), kept(PAIRS + 2, HALO, LANES, dtype=BF16)],
        [VMEM] * 2,
    )(dpre, taps)
    back = lax.ppermute(rim, "seq", [(i, i - 2) for i in range(2, n_seq)])
    keepx, keepbc, keepstep, give = call(
        swap_body,
        [
            kept(ROWS, HALF, dtype=BF16),
            kept(ROWS, 2 * LANES),
            kept(HEADS, ROWS),
            kept(PAIRS + 3, ROWS, LANES, dtype=BF16),
        ],
        [VMEM, VMEM, VMEM, FAR, VMEM],
    )(gx, gbc, back, gstep, side)
    came = lax.ppermute(give, "seq", [(i, i ^ 1) for i in range(n_seq)])
    gx, gbc, gstep = call(
        merge_body, [shape(ROWS, inner, dtype=BF16), shape(ROWS, 2 * LANES, dtype=BF16), shape(n, ROWS)], [VMEM] * 5
    )(keepx, keepbc, keepstep, came, side)
    weight, offset, bias, rate, skip = call(
        unpack_body,
        [shape(4, inner + 2 * LANES), shape(inner + 2 * LANES), shape(n), shape(n), shape(n)],
        [VMEM],
    )(part)
    return gx[None], gbc[None], gstep[None], weight, offset, bias, rate, skip


def solution(mesh):
    return jax.shard_map(
        compute,
        mesh=mesh,
        in_specs=(
            P("dp", "seq", None),
            P("dp", "seq", None),
            P("dp", None, "seq"),
            P(),
            P(),
            P(),
            P(),
            P(),
            P("dp", "seq", None),
        ),
        out_specs=(
            P("dp", "seq", None),
            P("dp", "seq", None),
            P("dp", None, "seq"),
            P(),
            P(),
            P(),
            P(),
            P(),
        ),
        check_vma=False,
    )
```

```python
import jax
import jax.numpy as jnp
from jax import lax
from jax.experimental import pallas as pl
from jax.experimental.pallas import tpu as pltpu
from jax.sharding import PartitionSpec as P


HIGH = lax.Precision.HIGHEST
F32 = jnp.float32
BF16 = jnp.bfloat16
ROWS = 128
LANES = 128
HALO = 8
PAIRS = 8
HEADS = 16
HALF = PAIRS * LANES
WIDE = 2 * LANES
SEG = 2 * ROWS
G_AT, B_AT, C_AT, STEP_AT = HALF, 2 * HALF, 2 * HALF + ROWS, 2 * HALF + 2 * ROWS
SIDE_AT = STEP_AT + 3 * HEADS
PACKED = SIDE_AT + 16
SENT = 2 * ROWS + 8
VMEM = pl.BlockSpec(memory_space=pltpu.VMEM)
FAR = pl.BlockSpec(memory_space=pltpu.VMEM)
SMEM = pl.BlockSpec(memory_space=pltpu.SMEM)
INTERPRET = False
NT = ((1,), (1,))
TN = ((0,), (0,))


def call(body, outs, ins, scratch=()):
    kernel = pl.pallas_call(
        body,
        out_shape=outs,
        in_specs=ins,
        out_specs=[VMEM] * len(outs),
        scratch_shapes=list(scratch),
        compiler_params=pltpu.CompilerParams(vmem_limit_bytes=16 << 20),
        interpret=INTERPRET,
    )
    if INTERPRET:
        return kernel
    return lambda *given: kernel(
        *(
            pltpu.with_memory_space_constraint(a, pltpu.VMEM if spec is VMEM else pltpu.HBM)
            for a, spec in zip(given, ins, strict=True)
        )
    )


def shape(*dims, dtype=F32):
    return jax.ShapeDtypeStruct(dims, dtype)


def far(*dims, dtype=F32):
    return shape(*dims, dtype=dtype) if INTERPRET else pltpu.HBM(dims, dtype)


def kept(*dims, dtype=F32):
    return shape(*dims, dtype=dtype) if INTERPRET else pltpu.VMEM(dims, dtype)


def dot(a, b, dims=((1,), (0,)), precision=None):
    return lax.dot_general(a, b, (dims, ((), ())), precision=precision, preferred_element_type=F32)


def iota(dims, axis):
    return lax.broadcasted_iota(jnp.int32, dims, axis)


def pack_body(x_ref, bc_ref, g_ref, step_ref, out_ref):
    bc = bc_ref[...]
    for q in range(2):
        for o in range(PAIRS):
            at = q * HALF + o * LANES
            out_ref[q, o * ROWS : (o + 1) * ROWS, :] = x_ref[:, at : at + LANES]
            out_ref[q, G_AT + o * ROWS : G_AT + (o + 1) * ROWS, :] = g_ref[:, at : at + LANES]
        out_ref[q, B_AT : B_AT + ROWS, :] = bc[:, :LANES]
        out_ref[q, C_AT : C_AT + ROWS, :] = bc[:, LANES:]
        rest = step_ref[q * HEADS : (q + 1) * HEADS, :]
        for k in range(3):
            piece = rest.astype(BF16)
            rest = rest - piece.astype(F32)
            out_ref[q, STEP_AT + k * HEADS : STEP_AT + (k + 1) * HEADS, :] = piece
        out_ref[q, SIDE_AT:, :] = jnp.full((16, LANES), float(q), F32).astype(BF16)


def tail_body(got_ref, out_ref):
    for o in range(PAIRS):
        out_ref[o, :, :] = got_ref[1, (o + 1) * ROWS - HALO : (o + 1) * ROWS, :]
    out_ref[PAIRS, :, :] = got_ref[1, B_AT + ROWS - HALO : B_AT + ROWS, :]
    out_ref[PAIRS + 1, :, :] = got_ref[1, C_AT + ROWS - HALO : C_AT + ROWS, :]


def head_rows(ref, second):
    rows = iota((2 * HEADS, LANES), 0) % HEADS
    out = jnp.zeros((2 * HEADS, LANES), F32)
    for h in range(HEADS):
        out = jnp.where(rows == h, jnp.where(second, ref[HEADS + h], ref[h]), out)
    return out


def steps_body(got_ref, weight_ref, offset_ref, bias_ref, rate_ref, skip_ref, rows_ref, cols_ref, taps_ref, side_ref, parts_ref):
    side = got_ref[0, SIDE_AT:, :].astype(F32)[:8]
    side_ref[...] = side
    second = side[:1] > 0.5
    offset = offset_ref[...].reshape(1, -1)
    inner = 2 * HALF
    for o in range(PAIRS):
        at = o * LANES
        lanes = slice(at, at + LANES)
        other = slice(HALF + at, HALF + at + LANES)
        taps_ref[:4, lanes] = jnp.where(second, weight_ref[:, other], weight_ref[:, lanes])
        taps_ref[4:5, lanes] = jnp.where(second, offset[:, other], offset[:, lanes])
    taps_ref[:4, HALF:] = weight_ref[:, inner:]
    taps_ref[4:5, HALF:] = offset[:, inner:]
    n = 2 * HEADS
    raw = [
        sum(got_ref[r, STEP_AT + k * HEADS : STEP_AT + (k + 1) * HEADS, :].astype(F32) for k in (2, 1, 0)) for r in range(2)
    ]
    second = jnp.broadcast_to(second, (n, LANES))
    raw = jnp.concatenate(raw, 0) + head_rows(bias_ref, second)
    step = jnp.maximum(raw, 0.0) + jnp.log1p(jnp.exp(-jnp.abs(raw)))
    rate = -jnp.exp(head_rows(rate_ref, second))
    upto = (iota((ROWS, ROWS), 0) <= iota((ROWS, ROWS), 1)).astype(F32)
    cumul = dot(rate * step, upto, precision=HIGH)
    weight = jnp.exp(cumul[:, ROWS - 1 :] - cumul) * step
    fade = jnp.exp(cumul)
    stack = jnp.concatenate([cumul, step, weight, fade], 0)
    rows_ref[: 4 * n, :] = stack
    rows_ref[4 * n : 5 * n, :] = jax.nn.sigmoid(raw)
    rows_ref[5 * n : 6 * n, :] = rate
    rows_ref[6 * n :, :] = head_rows(skip_ref, second)
    cols_ref[...] = stack.T
    for k, value in enumerate((weight, fade)):
        split = [value]
        for _ in range(2):
            split.append(split[-1] - split[-1].astype(BF16).astype(F32))
        for r in range(2):
            for c in range(HALF // WIDE):
                at = r * HEADS + 4 * c
                rows = [piece[at : at + 4] for piece in split] + [jnp.zeros((4, ROWS), F32)]
                parts_ref[k, r, c] = jnp.concatenate(rows, 0).astype(BF16)


def spreader():
    part, head = iota((16, WIDE), 0), iota((16, WIDE), 1) // 64
    return jnp.where((part % 4 == head) & (part < 12), 1.0, 0.0).astype(BF16)


def beside(first, second):
    return jnp.concatenate([first, second], 1)


def head_of(r, o):
    return r * HEADS + 2 * o


def fill(ext_ref, got_ref, halo_ref):
    for o in range(PAIRS + 2):
        at = o * ROWS if o < PAIRS else B_AT + (o - PAIRS) * ROWS
        ext_ref[o, :HALO, :] = halo_ref[o].astype(F32)
        for r in range(2):
            ext_ref[o, HALO + r * ROWS : HALO + (r + 1) * ROWS, :] = got_ref[r, at : at + ROWS, :].astype(F32)


def preact(ext_ref, taps_ref, o, first=0, count=SEG):
    lanes = slice(o * LANES, (o + 1) * LANES)
    acc = taps_ref[4:5, lanes]
    for k in range(4):
        acc = acc + taps_ref[k : k + 1, lanes] * ext_ref[o, pl.ds(HALO - 3 + k + first, count), :]
    return acc


def pair_column(cols_ref, which, r, o, left):
    at = which * 2 * HEADS + head_of(r, o)
    a = jnp.broadcast_to(cols_ref[:, at : at + 1], (ROWS, LANES))
    b = jnp.broadcast_to(cols_ref[:, at + 1 : at + 2], (ROWS, LANES))
    return jnp.where(left, a, b)


def decay_of(tail):
    tail = tail.astype(F32)
    return tail[0:1, :] + tail[1:2, :]


def decay_rows(total):
    high = total.astype(BF16).astype(F32)
    row = iota((8, LANES), 0)
    return jnp.where(row == 0, high, jnp.where(row == 1, total - high, 0.0)).astype(BF16)


def first_body(got_ref, halo_ref, taps_ref, parts_ref, bcact_ref, near_ref, send_ref, ext_ref):
    fill(ext_ref, got_ref, halo_ref)
    pre = beside(preact(ext_ref, taps_ref, PAIRS), preact(ext_ref, taps_ref, PAIRS + 1))
    bc = pre * jax.nn.sigmoid(pre)
    bcact_ref[...] = bc.astype(BF16)
    bc = bc.astype(BF16).astype(F32)
    b_t = [bc[r * ROWS : (r + 1) * ROWS, :LANES].T.astype(BF16) for r in range(2)]
    c_t = [bc[r * ROWS : (r + 1) * ROWS, LANES:].T.astype(BF16) for r in range(2)]
    over = spreader()
    for c in range(HALF // WIDE):
        ends, backs, totals = [], [], []
        g_at = G_AT + 2 * c * ROWS
        for r in range(2):
            pre = beside(*(preact(ext_ref, taps_ref, 2 * c + k, r * ROWS, ROWS) for k in range(2)))
            act = (pre * jax.nn.sigmoid(pre)).astype(BF16).astype(F32)
            fade = dot(parts_ref[1, r, c], over, TN)
            xw = (act * dot(parts_ref[0, r, c], over, TN)).astype(BF16)
            g = beside(got_ref[r, g_at : g_at + ROWS, :], got_ref[r, g_at + ROWS : g_at + 2 * ROWS, :])
            gw = (g.astype(F32) * fade).astype(BF16)
            ends.append(dot(b_t[r], xw))
            backs.append(dot(c_t[r], gw))
            totals.append(fade[ROWS - 1 :, :])
        end = totals[1] * ends[0] + ends[1]
        back = backs[0] + totals[0] * backs[1]
        total = totals[0] * totals[1]
        for k in range(2):
            o, lanes = 2 * c + k, slice(k * LANES, (k + 1) * LANES)
            near_ref[o, :ROWS, :] = ends[0][:, lanes].astype(BF16)
            near_ref[o, ROWS:, :] = backs[1][:, lanes].astype(BF16)
            send_ref[o, :ROWS, :] = end[:, lanes].astype(BF16)
            send_ref[o, ROWS : 2 * ROWS, :] = back[:, lanes].astype(BF16)
            send_ref[o, 2 * ROWS :, :] = decay_rows(total[:, lanes])


def scan_body(got_ref, out_ref):
    count = got_ref.shape[0]
    state = jnp.zeros((ROWS, LANES), F32)
    for j in range(count):
        out_ref[j, :ROWS, :] = state.astype(BF16)
        state = decay_of(got_ref[j, 2 * ROWS :, :]) * state + got_ref[j, :ROWS, :].astype(F32)
    state = jnp.zeros((ROWS, LANES), F32)
    for j in range(count - 1, -1, -1):
        out_ref[j, ROWS:, :] = state.astype(BF16)
        state = decay_of(got_ref[j, 2 * ROWS :, :]) * state + got_ref[j, ROWS : 2 * ROWS, :].astype(F32)


def inner_body(
    got_ref, halo_ref, taps_ref, rows_ref, cols_ref, bcact_ref,
    dx_ref, slope_ref, xw_ref, gw_ref, dbc_ref, slope2_ref, row_ref, ext_ref,
):
    n = 2 * HEADS
    fill(ext_ref, got_ref, halo_ref)
    pre = beside(preact(ext_ref, taps_ref, PAIRS), preact(ext_ref, taps_ref, PAIRS + 1))
    gate = jax.nn.sigmoid(pre)
    slope2_ref[...] = gate * (1.0 + pre * (1.0 - gate))
    causal = iota((ROWS, ROWS), 0) <= iota((ROWS, ROWS), 1)
    left = iota((ROWS, LANES), 1) < 64
    ones = jnp.ones((8, ROWS), BF16)
    b = [bcact_ref[r * ROWS : (r + 1) * ROWS, :LANES] for r in range(2)]
    c = [bcact_ref[r * ROWS : (r + 1) * ROWS, LANES:] for r in range(2)]
    scores = [dot(b[r], c[r], NT) for r in range(2)]
    dscores = [jnp.zeros((ROWS, ROWS), F32) for _ in range(2)]
    for o in range(PAIRS):
        lanes = slice(o * LANES, (o + 1) * LANES)
        pre = preact(ext_ref, taps_ref, o)
        gate = jax.nn.sigmoid(pre)
        slope_ref[:, lanes] = (gate * (1.0 + pre * (1.0 - gate))).astype(BF16)
        whole = (pre * gate).astype(BF16)
        for r in range(2):
            h = head_of(r, o)
            rows = slice(r * ROWS, (r + 1) * ROWS)
            act = whole[rows]
            wide = got_ref[r, G_AT + o * ROWS : G_AT + (o + 1) * ROWS, :].astype(F32)
            xw_ref[rows, lanes] = (act.astype(F32) * pair_column(cols_ref, 2, r, o, left)).astype(BF16)
            gw_ref[rows, lanes] = (wide * pair_column(cols_ref, 3, r, o, left)).astype(BF16)
            skip = jnp.where(left[:1], rows_ref[6 * n + h : 6 * n + h + 1, :], rows_ref[6 * n + h + 1 : 6 * n + h + 2, :])
            dx = skip * wide
            both = jnp.sum(act.astype(F32) * wide, 0, keepdims=True)
            row_ref[2 * n + h : 2 * n + h + 1, :] = jnp.where(left[:1], both, 0.0)
            row_ref[2 * n + h + 1 : 2 * n + h + 2, :] = jnp.where(left[:1], 0.0, both)
            for k in range(2):
                own = jnp.where(left if k == 0 else ~left, wide, 0.0).astype(BF16)
                gap = rows_ref[h + k : h + k + 1, :] - cols_ref[:, h + k : h + k + 1]
                fall = jnp.exp(jnp.where(causal, gap, -1e30)) * cols_ref[:, n + h + k : n + h + k + 1]
                mixing = scores[r] * fall
                dmix = dot(act, own, NT).astype(BF16).astype(F32)
                dscores[r] = dscores[r] + dmix * fall
                both = (dmix * mixing).astype(BF16)
                row_ref[h + k : h + k + 1, :] = dot(ones, both)[:1]
                row_ref[n + h + k : n + h + k + 1, :] = dot(ones, both, NT)[:1]
                dx = dx + dot(mixing.astype(BF16), own)
            dx_ref[rows, lanes] = dx.astype(BF16)
    for r in range(2):
        ds = dscores[r].astype(BF16)
        dbc_ref[r * ROWS : (r + 1) * ROWS, :LANES] = dot(ds, c[r])
        dbc_ref[r * ROWS : (r + 1) * ROWS, LANES:] = dot(ds, b[r], TN)


def tap_sums(dpre_ref, ext_ref, o):
    dpre = dpre_ref[o, HALO : HALO + SEG, :]
    sums = [jnp.sum(dpre * ext_ref[o, pl.ds(HALO - 3 + k, SEG), :], 0, keepdims=True) for k in range(4)]
    return sums + [jnp.sum(dpre, 0, keepdims=True)]


def last_body(
    got_ref, halo_ref, rows_ref, cols_ref, parts_ref, bcact_ref, side_ref, states_ref,
    near_ref, dx_ref, slope_ref, xw_ref, gw_ref, dbc_ref, slope2_ref, row_ref,
    dpre_ref, gstep_ref, sent_ref, ext_ref, acc_ref, state_ref, later_ref, sums_ref, part_ref,
):
    n = 2 * HEADS
    left = iota((1, LANES), 1) < 64
    quarter = iota((1, WIDE), 1) // 64
    b = [bcact_ref[r * ROWS : (r + 1) * ROWS, :LANES] for r in range(2)]
    c = [bcact_ref[r * ROWS : (r + 1) * ROWS, LANES:] for r in range(2)]
    fill(ext_ref, got_ref, halo_ref)
    part_ref[...] = jnp.zeros(part_ref.shape, F32)
    pad = jnp.zeros((PAIRS + 2, HALO, LANES), F32)
    dpre_ref[:, :HALO, :] = pad
    dpre_ref[:, HALO + SEG :, :] = pad
    over = spreader()
    for m in range(HALF // WIDE):
        lanes = slice(m * WIDE, (m + 1) * WIDE)
        total = []
        for r in range(2):
            h = 3 * n + r * HEADS + 4 * m
            row = cols_ref[ROWS - 1 :, h : h + 1]
            for k in range(1, 4):
                row = jnp.where(quarter >= k, cols_ref[ROWS - 1 :, h + k : h + k + 1], row)
            total.append(row)
        state, later, near, near_later = (
            beside(ref[2 * m, rows, :], ref[2 * m + 1, rows, :])
            for ref in (states_ref, near_ref)
            for rows in (slice(0, ROWS), slice(ROWS, 2 * ROWS))
        )
        states = [state, (total[0] * state.astype(F32) + near.astype(F32)).astype(BF16)]
        laters = [(total[1] * later.astype(F32) + near_later.astype(F32)).astype(BF16), later]
        for r in range(2):
            rows = slice(r * ROWS, (r + 1) * ROWS)
            state_ref[r, :, lanes] = states[r]
            later_ref[r, :, lanes] = laters[r]
            xw = xw_ref[rows, lanes].astype(F32)
            sums_ref[rows, lanes] = (dot(c[r], states[r]) * gw_ref[rows, lanes].astype(F32)).astype(BF16)
            dxw = dot(b[r], laters[r])
            sums_ref[rows, HALF + m * WIDE : HALF + (m + 1) * WIDE] = (dxw * xw).astype(BF16)
            both = jnp.sum(states[r].astype(F32) * laters[r].astype(F32), 0, keepdims=True)
            for k in range(2):
                h = head_of(r, 2 * m + k)
                mine = both[:, k * LANES : (k + 1) * LANES]
                acc_ref[h : h + 1, :] = jnp.where(left, mine, 0.0)
                acc_ref[h + 1 : h + 2, :] = jnp.where(left, 0.0, mine)
            dact = dx_ref[rows, lanes].astype(F32) + dot(parts_ref[0, r, m], over, TN) * dxw
            dact = dact * slope_ref[rows, lanes].astype(F32)
            for k in range(2):
                dpre_ref[2 * m + k, HALO + r * ROWS : HALO + (r + 1) * ROWS, :] = dact[:, k * LANES : (k + 1) * LANES]
    dpre2 = []
    for r in range(2):
        rows = slice(r * ROWS, (r + 1) * ROWS)
        dpre2.append(beside(dot(xw_ref[rows, :], later_ref[r], NT), dot(gw_ref[rows, :], state_ref[r], NT)))
    dpre2 = (dbc_ref[...] + jnp.concatenate(dpre2, 0)) * slope2_ref[...]
    for k in range(2):
        dpre_ref[PAIRS + k, HALO : HALO + SEG, :] = dpre2[:, k * LANES : (k + 1) * LANES]
    for o in range(PAIRS + 2):
        sums = tap_sums(dpre_ref, ext_ref, o)
        for k in range(5):
            if o < PAIRS:
                part_ref[o, k : k + 1, :] = sums[k]
            else:
                part_ref[k, 5 + o - PAIRS : 6 + o - PAIRS, :] = sums[k]
    lane = iota((16, LANES), 1)
    pick = [jnp.where(lane == h, 1.0, 0.0).astype(BF16) for h in range(n)]
    pick = jnp.concatenate([p for p in pick for _ in range(4)], 0)
    by_head = dot(sums_ref[...], pick)
    by_head = [by_head[r * ROWS : (r + 1) * ROWS].T for r in range(2)]
    entered = jnp.concatenate([t[:HEADS] for t in by_head], 0)
    ended = jnp.concatenate([t[HEADS:n] for t in by_head], 0)
    step = rows_ref[n : 2 * n, :]
    gate = rows_ref[4 * n : 5 * n, :]
    rate = rows_ref[5 * n : 6 * n, :]
    total = rows_ref[3 * n : 4 * n, ROWS - 1 :]
    at_t = row_ref[:n, :]
    at_s = row_ref[n : 2 * n, :]
    at_end = jnp.sum(ended, 1, keepdims=True) + total * jnp.sum(acc_ref[...], 1, keepdims=True)
    final = iota((n, ROWS), 1) == ROWS - 1
    dcumul = at_t - at_s + entered - ended + jnp.where(final, at_end, 0.0)
    onward = (iota((ROWS, ROWS), 0) >= iota((ROWS, ROWS), 1)).astype(F32)
    ddecay = dot(dcumul, onward, precision=HIGH)
    dstep = ((at_s + ended) / step + ddecay * rate) * gate
    gstep_ref[...] = dstep
    dbias = jnp.sum(dstep, 1, keepdims=True)
    drate = jnp.sum(ddecay * rate * step, 1, keepdims=True)
    dskip = jnp.sum(row_ref[2 * n :, :], 1, keepdims=True)
    second = jnp.broadcast_to(side_ref[:1] > 0.5, (n, LANES))
    at = iota((n, LANES), 1) - iota((n, LANES), 0) % HEADS - jnp.where(second, HEADS, 0)
    placed = jnp.where(at == 0, dbias, jnp.where(at == n, drate, jnp.where(at == 2 * n, dskip, 0.0)))
    part_ref[0, 7:8, :] = jnp.sum(placed, 0, keepdims=True)
    for o in range(PAIRS):
        sent_ref[o] = part_ref[o].astype(BF16)


def input_body(dpre_ref, taps_ref, gx_ref, gbc_ref, rim_ref):
    for o in range(PAIRS + 2):
        lanes = slice(o * LANES, (o + 1) * LANES)
        own = jnp.zeros((SEG, LANES), F32)
        rim = jnp.zeros((HALO, LANES), F32)
        for k in range(4):
            tap = taps_ref[k : k + 1, lanes]
            own = own + tap * dpre_ref[o, pl.ds(HALO + 3 - k, SEG), :]
            rim = rim + tap * dpre_ref[o, pl.ds(HALO - k, HALO), :]
        rim_ref[o, :, :] = rim.astype(BF16)
        if o < PAIRS:
            gx_ref[:, lanes] = own.astype(BF16)
        else:
            gbc_ref[:, (o - PAIRS) * LANES : (o - PAIRS + 1) * LANES] = own


def swap_body(gx_ref, gbc_ref, back_ref, gstep_ref, side_ref, keepx_ref, keepbc_ref, keepstep_ref, give_ref):
    second = side_ref[:1] > 0.5
    whole = jnp.broadcast_to(second, (ROWS, LANES))
    last = iota((HALO, LANES), 0) >= HALO - 3
    for o in range(PAIRS + 2):
        lanes = slice(o * LANES, (o + 1) * LANES)
        came = pltpu.roll(back_ref[o].astype(F32), HALO - 3, 0)
        came = jnp.where(last, came, 0.0)
        came = jnp.concatenate([jnp.zeros((ROWS - HALO, LANES), F32), came], 0)
        if o < PAIRS:
            first, then = gx_ref[:ROWS, lanes].astype(F32), gx_ref[ROWS:, lanes].astype(F32) + came
            keepx_ref[:, lanes] = jnp.where(whole, then, first).astype(BF16)
        else:
            mine = slice((o - PAIRS) * LANES, (o - PAIRS + 1) * LANES)
            first, then = gbc_ref[:ROWS, mine], gbc_ref[ROWS:, mine] + came
            keepbc_ref[:, mine] = jnp.where(whole, then, first)
        give_ref[o, :, :] = jnp.where(whole, first, then).astype(BF16)
    first, then = gstep_ref[:HEADS, :], gstep_ref[HEADS:, :]
    keepstep_ref[...] = jnp.where(whole[:HEADS], then, first)
    given = jnp.where(whole[:HEADS], first, then)
    high = given.astype(BF16)
    give_ref[PAIRS + 2, :HEADS, :] = high
    give_ref[PAIRS + 2, HEADS : 2 * HEADS, :] = (given - high.astype(F32)).astype(BF16)
    give_ref[PAIRS + 2, 2 * HEADS :, :] = jnp.zeros((ROWS - 2 * HEADS, LANES), BF16)


def merge_body(keepx_ref, keepbc_ref, keepstep_ref, came_ref, side_ref, gx_ref, gbc_ref, gstep_ref):
    second = side_ref[:1] > 0.5
    whole = jnp.broadcast_to(second, (ROWS, LANES))
    for o in range(PAIRS):
        lanes = slice(o * LANES, (o + 1) * LANES)
        mine, other = keepx_ref[:, lanes].astype(F32), came_ref[o].astype(F32)
        gx_ref[:, lanes] = jnp.where(whole, other, mine).astype(BF16)
        gx_ref[:, HALF + o * LANES : HALF + (o + 1) * LANES] = jnp.where(whole, mine, other).astype(BF16)
    for k in range(2):
        lanes = slice(k * LANES, (k + 1) * LANES)
        gbc_ref[:, lanes] = (keepbc_ref[:, lanes] + came_ref[PAIRS + k].astype(F32)).astype(BF16)
    mine = keepstep_ref[...]
    other = came_ref[PAIRS + 2, :HEADS, :].astype(F32) + came_ref[PAIRS + 2, HEADS : 2 * HEADS, :].astype(F32)
    gstep_ref[:HEADS, :] = jnp.where(whole[:HEADS], other, mine)
    gstep_ref[HEADS:, :] = jnp.where(whole[:HEADS], mine, other)


def spread_body(in_ref, out_ref, *, scale):
    total = in_ref[0].astype(F32)
    for j in range(1, in_ref.shape[0]):
        total = total + in_ref[j].astype(F32)
    total = (total * scale).astype(BF16)
    for j in range(out_ref.shape[0]):
        out_ref[j] = total


def spread(x, count, scale):
    def body(in_ref, out_ref):
        spread_body(in_ref, out_ref, scale=scale)

    return call(body, [far(count, 8, LANES, dtype=BF16)], [VMEM])(x)[0]


def unpack_body(in_ref, weight_ref, offset_ref, bias_ref, rate_ref, skip_ref):
    pieces = [in_ref[j].astype(F32) for j in range(2 * PAIRS)]
    heads = pieces[0][7:8, :] + pieces[1][7:8, :]
    for k, ref in enumerate((bias_ref, rate_ref, skip_ref)):
        ref[...] = heads[:, k * 2 * HEADS : (k + 1) * 2 * HEADS].reshape(2 * HEADS)
    for k in range(2):
        for o in range(PAIRS):
            lanes = slice(k * HALF + o * LANES, k * HALF + (o + 1) * LANES)
            weight_ref[:, lanes] = pieces[2 * o + k][:4]
            offset_ref[lanes] = pieces[2 * o + k][4]
    for k in range(5):
        both = pieces[2 * k][5:7] + pieces[2 * k + 1][5:7]
        for m in range(2):
            lanes = slice(2 * HALF + m * LANES, 2 * HALF + (m + 1) * LANES)
            if k < 4:
                weight_ref[k : k + 1, lanes] = both[m : m + 1]
            else:
                offset_ref[lanes] = both[m]


def compute(
    mixer_input, state_input, step_raw, conv_weight, conv_bias, step_bias, log_rate, skip_gain, grad_out
):
    x, bc, step, g = mixer_input[0], state_input[0], step_raw[0], grad_out[0]
    n_seq, n_dp = lax.axis_size("seq"), lax.axis_size("dp")
    chips = n_seq // 2
    inner = 2 * HALF
    n = 2 * HEADS
    assert x.shape == (ROWS, inner) and bc.shape == (ROWS, 2 * LANES) and chips == PAIRS and step.shape[0] == n
    cores = [[2 * c, 2 * c + 1] for c in range(chips)]
    ring = [[2 * c + k for c in range(chips)] for k in range(2)]
    packed = call(pack_body, [shape(2, PACKED, LANES, dtype=BF16)], [FAR] * 4)(x, bc, g, step)[0]
    got = lax.all_to_all(packed, "seq", 0, 0, axis_index_groups=cores)
    tail = call(tail_body, [kept(PAIRS + 2, HALO, LANES, dtype=BF16)], [VMEM])(got)[0]
    halo = lax.ppermute(tail, "seq", [(i, i + 2) for i in range(n_seq - 2)])
    by_row, by_col, taps, side, parts = call(
        steps_body,
        [
            kept(7 * n, ROWS),
            kept(ROWS, 4 * n),
            kept(5, HALF + 2 * LANES),
            kept(8, LANES),
            kept(2, 2, HALF // WIDE, 16, ROWS, dtype=BF16),
        ],
        [VMEM, FAR, FAR, SMEM, SMEM, SMEM],
    )(got, conv_weight, conv_bias, step_bias, log_rate, skip_gain)
    ext = [pltpu.VMEM((PAIRS + 2, SEG + HALO, LANES), F32)]
    bc_act, near, send = call(
        first_body,
        [
            kept(SEG, 2 * LANES, dtype=BF16),
            kept(PAIRS, 2 * ROWS, LANES, dtype=BF16),
            far(PAIRS, SENT, LANES, dtype=BF16),
        ],
        [VMEM] * 4,
        ext,
    )(got, halo, taps, parts)
    sent = lax.all_to_all(send, "seq", 0, 0, axis_index_groups=ring)
    dx, slope, xw, gw, dbc, slope2, row = call(
        inner_body,
        [
            far(SEG, HALF, dtype=BF16),
            far(SEG, HALF, dtype=BF16),
            far(SEG, HALF, dtype=BF16),
            far(SEG, HALF, dtype=BF16),
            far(SEG, 2 * LANES),
            far(SEG, 2 * LANES),
            far(3 * n, ROWS),
        ],
        [VMEM] * 6,
        ext,
    )(got, halo, taps, by_row, by_col, bc_act)
    scanned = call(scan_body, [shape(chips, 2 * ROWS, LANES, dtype=BF16)], [VMEM])(sent)[0]
    states = lax.all_to_all(scanned, "seq", 0, 0, axis_index_groups=ring)
    dpre, gstep, part = call(
        last_body,
        [kept(PAIRS + 2, SEG + 2 * HALO, LANES), far(n, ROWS), far(PAIRS, 8, LANES, dtype=BF16)],
        [VMEM] * 13 + [FAR] * 3,
        ext
        + [
            pltpu.VMEM((n, ROWS), F32),
            pltpu.VMEM((2, ROWS, HALF), BF16),
            pltpu.VMEM((2, ROWS, HALF), BF16),
            pltpu.VMEM((SEG, 2 * HALF), BF16),
            pltpu.VMEM((PAIRS, 8, LANES), F32),
        ],
    )(got, halo, by_row, by_col, parts, bc_act, side, states, near, dx, slope, xw, gw, dbc, slope2, row)
    part = lax.all_to_all(part, "seq", 0, 0, axis_index_groups=ring)
    part = spread(part, n_dp, 1.0)
    part = lax.all_to_all(part, "dp", 0, 0)
    part = spread(part, n_seq, 1.0 / n_dp)
    part = lax.all_to_all(part, "seq", 0, 0)
    gx, gbc, rim = call(
        input_body,
        [kept(SEG, HALF, dtype=BF16), kept(SEG, 2 * LANES), kept(PAIRS + 2, HALO, LANES, dtype=BF16)],
        [VMEM] * 2,
    )(dpre, taps)
    back = lax.ppermute(rim, "seq", [(i, i - 2) for i in range(2, n_seq)])
    keepx, keepbc, keepstep, give = call(
        swap_body,
        [
            kept(ROWS, HALF, dtype=BF16),
            kept(ROWS, 2 * LANES),
            kept(HEADS, ROWS),
            kept(PAIRS + 3, ROWS, LANES, dtype=BF16),
        ],
        [VMEM, VMEM, VMEM, FAR, VMEM],
    )(gx, gbc, back, gstep, side)
    came = lax.ppermute(give, "seq", [(i, i ^ 1) for i in range(n_seq)])
    gx, gbc, gstep = call(
        merge_body, [shape(ROWS, inner, dtype=BF16), shape(ROWS, 2 * LANES, dtype=BF16), shape(n, ROWS)], [VMEM] * 5
    )(keepx, keepbc, keepstep, came, side)
    weight, offset, bias, rate, skip = call(
        unpack_body,
        [shape(4, inner + 2 * LANES), shape(inner + 2 * LANES), shape(n), shape(n), shape(n)],
        [VMEM],
    )(part)
    return gx[None], gbc[None], gstep[None], weight, offset, bias, rate, skip


def solution(mesh):
    return jax.shard_map(
        compute,
        mesh=mesh,
        in_specs=(
            P("dp", "seq", None),
            P("dp", "seq", None),
            P("dp", None, "seq"),
            P(),
            P(),
            P(),
            P(),
            P(),
            P("dp", "seq", None),
        ),
        out_specs=(
            P("dp", "seq", None),
            P("dp", "seq", None),
            P("dp", None, "seq"),
            P(),
            P(),
            P(),
            P(),
            P(),
        ),
        check_vma=False,
    )
```

```python
import jax
import jax.numpy as jnp
from jax import lax
from jax.experimental import pallas as pl
from jax.experimental.pallas import tpu as pltpu
from jax.sharding import PartitionSpec as P


HIGH = lax.Precision.HIGHEST
F32 = jnp.float32
BF16 = jnp.bfloat16
ROWS = 128
LANES = 128
HALO = 8
PAIRS = 8
HEADS = 16
HALF = PAIRS * LANES
WIDE = 2 * LANES
SEG = 2 * ROWS
G_AT, B_AT, C_AT, STEP_AT = HALF, 2 * HALF, 2 * HALF + ROWS, 2 * HALF + 2 * ROWS
SIDE_AT = STEP_AT + 3 * HEADS
PACKED = SIDE_AT + 16
SENT = 2 * ROWS + 8
VMEM = pl.BlockSpec(memory_space=pltpu.VMEM)
FAR = pl.BlockSpec(memory_space=pltpu.VMEM)
SMEM = pl.BlockSpec(memory_space=pltpu.SMEM)
INTERPRET = False
NT = ((1,), (1,))
TN = ((0,), (0,))


def call(body, outs, ins, scratch=()):
    kernel = pl.pallas_call(
        body,
        out_shape=outs,
        in_specs=ins,
        out_specs=[VMEM] * len(outs),
        scratch_shapes=list(scratch),
        compiler_params=pltpu.CompilerParams(vmem_limit_bytes=16 << 20),
        interpret=INTERPRET,
    )
    if INTERPRET:
        return kernel
    return lambda *given: kernel(
        *(
            pltpu.with_memory_space_constraint(a, pltpu.VMEM if spec is VMEM else pltpu.HBM)
            for a, spec in zip(given, ins, strict=True)
        )
    )


def shape(*dims, dtype=F32):
    return jax.ShapeDtypeStruct(dims, dtype)


def far(*dims, dtype=F32):
    return shape(*dims, dtype=dtype) if INTERPRET else pltpu.HBM(dims, dtype)


def kept(*dims, dtype=F32):
    return shape(*dims, dtype=dtype) if INTERPRET else pltpu.VMEM(dims, dtype)


def dot(a, b, dims=((1,), (0,)), precision=None):
    return lax.dot_general(a, b, (dims, ((), ())), precision=precision, preferred_element_type=F32)


def iota(dims, axis):
    return lax.broadcasted_iota(jnp.int32, dims, axis)


def pack_body(x_ref, bc_ref, g_ref, step_ref, out_ref):
    bc = bc_ref[...]
    for q in range(2):
        for o in range(PAIRS):
            at = q * HALF + o * LANES
            out_ref[q, o * ROWS : (o + 1) * ROWS, :] = x_ref[:, at : at + LANES]
            out_ref[q, G_AT + o * ROWS : G_AT + (o + 1) * ROWS, :] = g_ref[:, at : at + LANES]
        out_ref[q, B_AT : B_AT + ROWS, :] = bc[:, :LANES]
        out_ref[q, C_AT : C_AT + ROWS, :] = bc[:, LANES:]
        rest = step_ref[q * HEADS : (q + 1) * HEADS, :]
        for k in range(3):
            piece = rest.astype(BF16)
            rest = rest - piece.astype(F32)
            out_ref[q, STEP_AT + k * HEADS : STEP_AT + (k + 1) * HEADS, :] = piece
        out_ref[q, SIDE_AT:, :] = jnp.full((16, LANES), float(q), F32).astype(BF16)


def tail_body(got_ref, out_ref):
    for o in range(PAIRS):
        out_ref[o, :, :] = got_ref[1, (o + 1) * ROWS - HALO : (o + 1) * ROWS, :]
    out_ref[PAIRS, :, :] = got_ref[1, B_AT + ROWS - HALO : B_AT + ROWS, :]
    out_ref[PAIRS + 1, :, :] = got_ref[1, C_AT + ROWS - HALO : C_AT + ROWS, :]


def head_rows(ref, second):
    rows = iota((2 * HEADS, LANES), 0) % HEADS
    out = jnp.zeros((2 * HEADS, LANES), F32)
    for h in range(HEADS):
        out = jnp.where(rows == h, jnp.where(second, ref[HEADS + h], ref[h]), out)
    return out


def steps_body(got_ref, weight_ref, offset_ref, bias_ref, rate_ref, skip_ref, rows_ref, cols_ref, taps_ref, side_ref, parts_ref):
    side = got_ref[0, SIDE_AT:, :].astype(F32)[:8]
    side_ref[...] = side
    second = side[:1] > 0.5
    offset = offset_ref[...].reshape(1, -1)
    inner = 2 * HALF
    for o in range(PAIRS):
        at = o * LANES
        lanes = slice(at, at + LANES)
        other = slice(HALF + at, HALF + at + LANES)
        taps_ref[:4, lanes] = jnp.where(second, weight_ref[:, other], weight_ref[:, lanes])
        taps_ref[4:5, lanes] = jnp.where(second, offset[:, other], offset[:, lanes])
    taps_ref[:4, HALF:] = weight_ref[:, inner:]
    taps_ref[4:5, HALF:] = offset[:, inner:]
    n = 2 * HEADS
    raw = [
        sum(got_ref[r, STEP_AT + k * HEADS : STEP_AT + (k + 1) * HEADS, :].astype(F32) for k in (2, 1, 0)) for r in range(2)
    ]
    second = jnp.broadcast_to(second, (n, LANES))
    raw = jnp.concatenate(raw, 0) + head_rows(bias_ref, second)
    step = jnp.maximum(raw, 0.0) + jnp.log1p(jnp.exp(-jnp.abs(raw)))
    rate = -jnp.exp(head_rows(rate_ref, second))
    upto = (iota((ROWS, ROWS), 0) <= iota((ROWS, ROWS), 1)).astype(F32)
    cumul = dot(rate * step, upto, precision=HIGH)
    weight = jnp.exp(cumul[:, ROWS - 1 :] - cumul) * step
    fade = jnp.exp(cumul)
    stack = jnp.concatenate([cumul, step, weight, fade], 0)
    rows_ref[: 4 * n, :] = stack
    rows_ref[4 * n : 5 * n, :] = jax.nn.sigmoid(raw)
    rows_ref[5 * n : 6 * n, :] = rate
    rows_ref[6 * n :, :] = head_rows(skip_ref, second)
    cols_ref[...] = stack.T
    for k, value in enumerate((weight, fade)):
        split = [value]
        for _ in range(2):
            split.append(split[-1] - split[-1].astype(BF16).astype(F32))
        for r in range(2):
            for c in range(HALF // WIDE):
                at = r * HEADS + 4 * c
                rows = [piece[at : at + 4] for piece in split] + [jnp.zeros((4, ROWS), F32)]
                parts_ref[k, r, c] = jnp.concatenate(rows, 0).astype(BF16)


def spreader():
    part, head = iota((16, WIDE), 0), iota((16, WIDE), 1) // 64
    return jnp.where((part % 4 == head) & (part < 12), 1.0, 0.0).astype(BF16)


def beside(first, second):
    return jnp.concatenate([first, second], 1)


def head_of(r, o):
    return r * HEADS + 2 * o


def fill(ext_ref, got_ref, halo_ref):
    for o in range(PAIRS + 2):
        at = o * ROWS if o < PAIRS else B_AT + (o - PAIRS) * ROWS
        ext_ref[o, :HALO, :] = halo_ref[o].astype(F32)
        for r in range(2):
            ext_ref[o, HALO + r * ROWS : HALO + (r + 1) * ROWS, :] = got_ref[r, at : at + ROWS, :].astype(F32)


def preact(ext_ref, taps_ref, o, first=0, count=SEG):
    lanes = slice(o * LANES, (o + 1) * LANES)
    acc = taps_ref[4:5, lanes]
    for k in range(4):
        acc = acc + taps_ref[k : k + 1, lanes] * ext_ref[o, pl.ds(HALO - 3 + k + first, count), :]
    return acc


def pair_column(cols_ref, which, r, o, left):
    at = which * 2 * HEADS + head_of(r, o)
    a = jnp.broadcast_to(cols_ref[:, at : at + 1], (ROWS, LANES))
    b = jnp.broadcast_to(cols_ref[:, at + 1 : at + 2], (ROWS, LANES))
    return jnp.where(left, a, b)


def decay_of(tail):
    tail = tail.astype(F32)
    return tail[0:1, :] + tail[1:2, :]


def decay_rows(total):
    high = total.astype(BF16).astype(F32)
    row = iota((8, LANES), 0)
    return jnp.where(row == 0, high, jnp.where(row == 1, total - high, 0.0)).astype(BF16)


def first_body(got_ref, halo_ref, taps_ref, parts_ref, bcact_ref, near_ref, send_ref, ext_ref):
    fill(ext_ref, got_ref, halo_ref)
    pre = beside(preact(ext_ref, taps_ref, PAIRS), preact(ext_ref, taps_ref, PAIRS + 1))
    bc = pre * jax.nn.sigmoid(pre)
    bcact_ref[...] = bc.astype(BF16)
    bc = bc.astype(BF16).astype(F32)
    b_t = [bc[r * ROWS : (r + 1) * ROWS, :LANES].T.astype(BF16) for r in range(2)]
    c_t = [bc[r * ROWS : (r + 1) * ROWS, LANES:].T.astype(BF16) for r in range(2)]
    over = spreader()
    for c in range(HALF // WIDE):
        ends, backs, totals = [], [], []
        g_at = G_AT + 2 * c * ROWS
        for r in range(2):
            pre = beside(*(preact(ext_ref, taps_ref, 2 * c + k, r * ROWS, ROWS) for k in range(2)))
            act = (pre * jax.nn.sigmoid(pre)).astype(BF16).astype(F32)
            fade = dot(parts_ref[1, r, c], over, TN)
            xw = (act * dot(parts_ref[0, r, c], over, TN)).astype(BF16)
            g = beside(got_ref[r, g_at : g_at + ROWS, :], got_ref[r, g_at + ROWS : g_at + 2 * ROWS, :])
            gw = (g.astype(F32) * fade).astype(BF16)
            ends.append(dot(b_t[r], xw))
            backs.append(dot(c_t[r], gw))
            totals.append(fade[ROWS - 1 :, :])
        end = totals[1] * ends[0] + ends[1]
        back = backs[0] + totals[0] * backs[1]
        total = totals[0] * totals[1]
        for k in range(2):
            o, lanes = 2 * c + k, slice(k * LANES, (k + 1) * LANES)
            near_ref[o, :ROWS, :] = ends[0][:, lanes].astype(BF16)
            near_ref[o, ROWS:, :] = backs[1][:, lanes].astype(BF16)
            send_ref[o, :ROWS, :] = end[:, lanes].astype(BF16)
            send_ref[o, ROWS : 2 * ROWS, :] = back[:, lanes].astype(BF16)
            send_ref[o, 2 * ROWS :, :] = decay_rows(total[:, lanes])


def scan_body(got_ref, out_ref):
    count = got_ref.shape[0]
    state = jnp.zeros((ROWS, LANES), F32)
    for j in range(count):
        out_ref[j, :ROWS, :] = state.astype(BF16)
        state = decay_of(got_ref[j, 2 * ROWS :, :]) * state + got_ref[j, :ROWS, :].astype(F32)
    state = jnp.zeros((ROWS, LANES), F32)
    for j in range(count - 1, -1, -1):
        out_ref[j, ROWS:, :] = state.astype(BF16)
        state = decay_of(got_ref[j, 2 * ROWS :, :]) * state + got_ref[j, ROWS : 2 * ROWS, :].astype(F32)


def inner_body(
    got_ref, halo_ref, taps_ref, rows_ref, cols_ref, bcact_ref,
    dx_ref, slope_ref, xw_ref, gw_ref, dbc_ref, slope2_ref, row_ref, ext_ref,
):
    n = 2 * HEADS
    fill(ext_ref, got_ref, halo_ref)
    pre = beside(preact(ext_ref, taps_ref, PAIRS), preact(ext_ref, taps_ref, PAIRS + 1))
    gate = jax.nn.sigmoid(pre)
    slope2_ref[...] = (gate * (1.0 + pre * (1.0 - gate))).astype(BF16)
    causal = iota((ROWS, ROWS), 0) <= iota((ROWS, ROWS), 1)
    left = iota((ROWS, LANES), 1) < 64
    ones = jnp.ones((8, ROWS), BF16)
    b = [bcact_ref[r * ROWS : (r + 1) * ROWS, :LANES] for r in range(2)]
    c = [bcact_ref[r * ROWS : (r + 1) * ROWS, LANES:] for r in range(2)]
    scores = [dot(b[r], c[r], NT) for r in range(2)]
    dscores = [jnp.zeros((ROWS, ROWS), F32) for _ in range(2)]
    for o in range(PAIRS):
        lanes = slice(o * LANES, (o + 1) * LANES)
        pre = preact(ext_ref, taps_ref, o)
        gate = jax.nn.sigmoid(pre)
        slope_ref[:, lanes] = (gate * (1.0 + pre * (1.0 - gate))).astype(BF16)
        whole = (pre * gate).astype(BF16)
        for r in range(2):
            h = head_of(r, o)
            rows = slice(r * ROWS, (r + 1) * ROWS)
            act = whole[rows]
            wide = got_ref[r, G_AT + o * ROWS : G_AT + (o + 1) * ROWS, :].astype(F32)
            xw_ref[rows, lanes] = (act.astype(F32) * pair_column(cols_ref, 2, r, o, left)).astype(BF16)
            gw_ref[rows, lanes] = (wide * pair_column(cols_ref, 3, r, o, left)).astype(BF16)
            skip = jnp.where(left[:1], rows_ref[6 * n + h : 6 * n + h + 1, :], rows_ref[6 * n + h + 1 : 6 * n + h + 2, :])
            dx = skip * wide
            both = jnp.sum(act.astype(F32) * wide, 0, keepdims=True)
            row_ref[2 * n + h : 2 * n + h + 1, :] = jnp.where(left[:1], both, 0.0)
            row_ref[2 * n + h + 1 : 2 * n + h + 2, :] = jnp.where(left[:1], 0.0, both)
            for k in range(2):
                own = jnp.where(left if k == 0 else ~left, wide, 0.0).astype(BF16)
                gap = rows_ref[h + k : h + k + 1, :] - cols_ref[:, h + k : h + k + 1]
                fall = jnp.exp(jnp.where(causal, gap, -1e30)) * cols_ref[:, n + h + k : n + h + k + 1]
                mixing = scores[r] * fall
                dmix = dot(act, own, NT).astype(BF16).astype(F32)
                dscores[r] = dscores[r] + dmix * fall
                both = (dmix * mixing).astype(BF16)
                row_ref[h + k : h + k + 1, :] = dot(ones, both)[:1]
                row_ref[n + h + k : n + h + k + 1, :] = dot(ones, both, NT)[:1]
                dx = dx + dot(mixing.astype(BF16), own)
            dx_ref[rows, lanes] = dx.astype(BF16)
    for r in range(2):
        ds = dscores[r].astype(BF16)
        dbc_ref[r * ROWS : (r + 1) * ROWS, :LANES] = dot(ds, c[r]).astype(BF16)
        dbc_ref[r * ROWS : (r + 1) * ROWS, LANES:] = dot(ds, b[r], TN).astype(BF16)


def tap_sums(dpre_ref, ext_ref, o):
    dpre = dpre_ref[o, HALO : HALO + SEG, :]
    sums = [jnp.sum(dpre * ext_ref[o, pl.ds(HALO - 3 + k, SEG), :], 0, keepdims=True) for k in range(4)]
    return sums + [jnp.sum(dpre, 0, keepdims=True)]


def last_body(
    got_ref, halo_ref, rows_ref, cols_ref, parts_ref, bcact_ref, side_ref, states_ref,
    near_ref, dx_ref, slope_ref, xw_ref, gw_ref, dbc_ref, slope2_ref, row_ref,
    dpre_ref, gstep_ref, sent_ref, ext_ref, acc_ref, state_ref, later_ref, sums_ref, part_ref,
):
    n = 2 * HEADS
    left = iota((1, LANES), 1) < 64
    quarter = iota((1, WIDE), 1) // 64
    b = [bcact_ref[r * ROWS : (r + 1) * ROWS, :LANES] for r in range(2)]
    c = [bcact_ref[r * ROWS : (r + 1) * ROWS, LANES:] for r in range(2)]
    fill(ext_ref, got_ref, halo_ref)
    part_ref[...] = jnp.zeros(part_ref.shape, F32)
    pad = jnp.zeros((PAIRS + 2, HALO, LANES), F32)
    dpre_ref[:, :HALO, :] = pad
    dpre_ref[:, HALO + SEG :, :] = pad
    over = spreader()
    for m in range(HALF // WIDE):
        lanes = slice(m * WIDE, (m + 1) * WIDE)
        total = []
        for r in range(2):
            h = 3 * n + r * HEADS + 4 * m
            row = cols_ref[ROWS - 1 :, h : h + 1]
            for k in range(1, 4):
                row = jnp.where(quarter >= k, cols_ref[ROWS - 1 :, h + k : h + k + 1], row)
            total.append(row)
        state, later, near, near_later = (
            beside(ref[2 * m, rows, :], ref[2 * m + 1, rows, :])
            for ref in (states_ref, near_ref)
            for rows in (slice(0, ROWS), slice(ROWS, 2 * ROWS))
        )
        states = [state, (total[0] * state.astype(F32) + near.astype(F32)).astype(BF16)]
        laters = [(total[1] * later.astype(F32) + near_later.astype(F32)).astype(BF16), later]
        for r in range(2):
            rows = slice(r * ROWS, (r + 1) * ROWS)
            state_ref[r, :, lanes] = states[r]
            later_ref[r, :, lanes] = laters[r]
            xw = xw_ref[rows, lanes].astype(F32)
            sums_ref[rows, lanes] = (dot(c[r], states[r]) * gw_ref[rows, lanes].astype(F32)).astype(BF16)
            dxw = dot(b[r], laters[r])
            sums_ref[rows, HALF + m * WIDE : HALF + (m + 1) * WIDE] = (dxw * xw).astype(BF16)
            both = jnp.sum(states[r].astype(F32) * laters[r].astype(F32), 0, keepdims=True)
            for k in range(2):
                h = head_of(r, 2 * m + k)
                mine = both[:, k * LANES : (k + 1) * LANES]
                acc_ref[h : h + 1, :] = jnp.where(left, mine, 0.0)
                acc_ref[h + 1 : h + 2, :] = jnp.where(left, 0.0, mine)
            dact = dx_ref[rows, lanes].astype(F32) + dot(parts_ref[0, r, m], over, TN) * dxw
            dact = dact * slope_ref[rows, lanes].astype(F32)
            for k in range(2):
                dpre_ref[2 * m + k, HALO + r * ROWS : HALO + (r + 1) * ROWS, :] = dact[:, k * LANES : (k + 1) * LANES]
    dpre2 = []
    for r in range(2):
        rows = slice(r * ROWS, (r + 1) * ROWS)
        dpre2.append(beside(dot(xw_ref[rows, :], later_ref[r], NT), dot(gw_ref[rows, :], state_ref[r], NT)))
    dpre2 = (dbc_ref[...].astype(F32) + jnp.concatenate(dpre2, 0)) * slope2_ref[...].astype(F32)
    for k in range(2):
        dpre_ref[PAIRS + k, HALO : HALO + SEG, :] = dpre2[:, k * LANES : (k + 1) * LANES]
    for o in range(PAIRS + 2):
        sums = tap_sums(dpre_ref, ext_ref, o)
        for k in range(5):
            if o < PAIRS:
                part_ref[o, k : k + 1, :] = sums[k]
            else:
                part_ref[k, 5 + o - PAIRS : 6 + o - PAIRS, :] = sums[k]
    lane = iota((16, LANES), 1)
    pick = [jnp.where(lane == h, 1.0, 0.0).astype(BF16) for h in range(n)]
    pick = jnp.concatenate([p for p in pick for _ in range(4)], 0)
    by_head = dot(sums_ref[...], pick)
    by_head = [by_head[r * ROWS : (r + 1) * ROWS].T for r in range(2)]
    entered = jnp.concatenate([t[:HEADS] for t in by_head], 0)
    ended = jnp.concatenate([t[HEADS:n] for t in by_head], 0)
    step = rows_ref[n : 2 * n, :]
    gate = rows_ref[4 * n : 5 * n, :]
    rate = rows_ref[5 * n : 6 * n, :]
    total = rows_ref[3 * n : 4 * n, ROWS - 1 :]
    at_t = row_ref[:n, :]
    at_s = row_ref[n : 2 * n, :]
    at_end = jnp.sum(ended, 1, keepdims=True) + total * jnp.sum(acc_ref[...], 1, keepdims=True)
    final = iota((n, ROWS), 1) == ROWS - 1
    dcumul = at_t - at_s + entered - ended + jnp.where(final, at_end, 0.0)
    onward = (iota((ROWS, ROWS), 0) >= iota((ROWS, ROWS), 1)).astype(F32)
    ddecay = dot(dcumul, onward, precision=HIGH)
    dstep = ((at_s + ended) / step + ddecay * rate) * gate
    gstep_ref[...] = dstep
    dbias = jnp.sum(dstep, 1, keepdims=True)
    drate = jnp.sum(ddecay * rate * step, 1, keepdims=True)
    dskip = jnp.sum(row_ref[2 * n :, :], 1, keepdims=True)
    second = jnp.broadcast_to(side_ref[:1] > 0.5, (n, LANES))
    at = iota((n, LANES), 1) - iota((n, LANES), 0) % HEADS - jnp.where(second, HEADS, 0)
    placed = jnp.where(at == 0, dbias, jnp.where(at == n, drate, jnp.where(at == 2 * n, dskip, 0.0)))
    part_ref[0, 7:8, :] = jnp.sum(placed, 0, keepdims=True)
    for o in range(PAIRS):
        sent_ref[o] = part_ref[o].astype(BF16)


def input_body(dpre_ref, taps_ref, gx_ref, gbc_ref, rim_ref):
    for o in range(PAIRS + 2):
        lanes = slice(o * LANES, (o + 1) * LANES)
        own = jnp.zeros((SEG, LANES), F32)
        rim = jnp.zeros((HALO, LANES), F32)
        for k in range(4):
            tap = taps_ref[k : k + 1, lanes]
            own = own + tap * dpre_ref[o, pl.ds(HALO + 3 - k, SEG), :]
            rim = rim + tap * dpre_ref[o, pl.ds(HALO - k, HALO), :]
        rim_ref[o, :, :] = rim.astype(BF16)
        if o < PAIRS:
            gx_ref[:, lanes] = own.astype(BF16)
        else:
            gbc_ref[:, (o - PAIRS) * LANES : (o - PAIRS + 1) * LANES] = own


def swap_body(gx_ref, gbc_ref, back_ref, gstep_ref, side_ref, keepx_ref, keepbc_ref, keepstep_ref, give_ref):
    second = side_ref[:1] > 0.5
    whole = jnp.broadcast_to(second, (ROWS, LANES))
    last = iota((HALO, LANES), 0) >= HALO - 3
    for o in range(PAIRS + 2):
        lanes = slice(o * LANES, (o + 1) * LANES)
        came = pltpu.roll(back_ref[o].astype(F32), HALO - 3, 0)
        came = jnp.where(last, came, 0.0)
        came = jnp.concatenate([jnp.zeros((ROWS - HALO, LANES), F32), came], 0)
        if o < PAIRS:
            first, then = gx_ref[:ROWS, lanes].astype(F32), gx_ref[ROWS:, lanes].astype(F32) + came
            keepx_ref[:, lanes] = jnp.where(whole, then, first).astype(BF16)
        else:
            mine = slice((o - PAIRS) * LANES, (o - PAIRS + 1) * LANES)
            first, then = gbc_ref[:ROWS, mine], gbc_ref[ROWS:, mine] + came
            keepbc_ref[:, mine] = jnp.where(whole, then, first)
        give_ref[o, :, :] = jnp.where(whole, first, then).astype(BF16)
    first, then = gstep_ref[:HEADS, :], gstep_ref[HEADS:, :]
    keepstep_ref[...] = jnp.where(whole[:HEADS], then, first)
    given = jnp.where(whole[:HEADS], first, then)
    high = given.astype(BF16)
    give_ref[PAIRS + 2, :HEADS, :] = high
    give_ref[PAIRS + 2, HEADS : 2 * HEADS, :] = (given - high.astype(F32)).astype(BF16)
    give_ref[PAIRS + 2, 2 * HEADS :, :] = jnp.zeros((ROWS - 2 * HEADS, LANES), BF16)


def merge_body(keepx_ref, keepbc_ref, keepstep_ref, came_ref, side_ref, gx_ref, gbc_ref, gstep_ref):
    second = side_ref[:1] > 0.5
    whole = jnp.broadcast_to(second, (ROWS, LANES))
    for o in range(PAIRS):
        lanes = slice(o * LANES, (o + 1) * LANES)
        mine, other = keepx_ref[:, lanes].astype(F32), came_ref[o].astype(F32)
        gx_ref[:, lanes] = jnp.where(whole, other, mine).astype(BF16)
        gx_ref[:, HALF + o * LANES : HALF + (o + 1) * LANES] = jnp.where(whole, mine, other).astype(BF16)
    for k in range(2):
        lanes = slice(k * LANES, (k + 1) * LANES)
        gbc_ref[:, lanes] = (keepbc_ref[:, lanes] + came_ref[PAIRS + k].astype(F32)).astype(BF16)
    mine = keepstep_ref[...]
    other = came_ref[PAIRS + 2, :HEADS, :].astype(F32) + came_ref[PAIRS + 2, HEADS : 2 * HEADS, :].astype(F32)
    gstep_ref[:HEADS, :] = jnp.where(whole[:HEADS], other, mine)
    gstep_ref[HEADS:, :] = jnp.where(whole[:HEADS], mine, other)


def spread_body(in_ref, out_ref, *, scale):
    total = in_ref[0].astype(F32)
    for j in range(1, in_ref.shape[0]):
        total = total + in_ref[j].astype(F32)
    total = (total * scale).astype(BF16)
    for j in range(out_ref.shape[0]):
        out_ref[j] = total


def spread(x, count, scale):
    def body(in_ref, out_ref):
        spread_body(in_ref, out_ref, scale=scale)

    return call(body, [far(count, 8, LANES, dtype=BF16)], [VMEM])(x)[0]


def unpack_body(in_ref, weight_ref, offset_ref, bias_ref, rate_ref, skip_ref):
    pieces = [in_ref[j].astype(F32) for j in range(2 * PAIRS)]
    heads = pieces[0][7:8, :] + pieces[1][7:8, :]
    for k, ref in enumerate((bias_ref, rate_ref, skip_ref)):
        ref[...] = heads[:, k * 2 * HEADS : (k + 1) * 2 * HEADS].reshape(2 * HEADS)
    for k in range(2):
        for o in range(PAIRS):
            lanes = slice(k * HALF + o * LANES, k * HALF + (o + 1) * LANES)
            weight_ref[:, lanes] = pieces[2 * o + k][:4]
            offset_ref[lanes] = pieces[2 * o + k][4]
    for k in range(5):
        both = pieces[2 * k][5:7] + pieces[2 * k + 1][5:7]
        for m in range(2):
            lanes = slice(2 * HALF + m * LANES, 2 * HALF + (m + 1) * LANES)
            if k < 4:
                weight_ref[k : k + 1, lanes] = both[m : m + 1]
            else:
                offset_ref[lanes] = both[m]


def compute(
    mixer_input, state_input, step_raw, conv_weight, conv_bias, step_bias, log_rate, skip_gain, grad_out
):
    x, bc, step, g = mixer_input[0], state_input[0], step_raw[0], grad_out[0]
    n_seq, n_dp = lax.axis_size("seq"), lax.axis_size("dp")
    chips = n_seq // 2
    inner = 2 * HALF
    n = 2 * HEADS
    assert x.shape == (ROWS, inner) and bc.shape == (ROWS, 2 * LANES) and chips == PAIRS and step.shape[0] == n
    cores = [[2 * c, 2 * c + 1] for c in range(chips)]
    ring = [[2 * c + k for c in range(chips)] for k in range(2)]
    packed = call(pack_body, [shape(2, PACKED, LANES, dtype=BF16)], [FAR] * 4)(x, bc, g, step)[0]
    got = lax.all_to_all(packed, "seq", 0, 0, axis_index_groups=cores)
    tail = call(tail_body, [kept(PAIRS + 2, HALO, LANES, dtype=BF16)], [VMEM])(got)[0]
    halo = lax.ppermute(tail, "seq", [(i, i + 2) for i in range(n_seq - 2)])
    by_row, by_col, taps, side, parts = call(
        steps_body,
        [
            kept(7 * n, ROWS),
            kept(ROWS, 4 * n),
            kept(5, HALF + 2 * LANES),
            kept(8, LANES),
            kept(2, 2, HALF // WIDE, 16, ROWS, dtype=BF16),
        ],
        [VMEM, FAR, FAR, SMEM, SMEM, SMEM],
    )(got, conv_weight, conv_bias, step_bias, log_rate, skip_gain)
    ext = [pltpu.VMEM((PAIRS + 2, SEG + HALO, LANES), F32)]
    bc_act, near, send = call(
        first_body,
        [
            kept(SEG, 2 * LANES, dtype=BF16),
            kept(PAIRS, 2 * ROWS, LANES, dtype=BF16),
            far(PAIRS, SENT, LANES, dtype=BF16),
        ],
        [VMEM] * 4,
        ext,
    )(got, halo, taps, parts)
    sent = lax.all_to_all(send, "seq", 0, 0, axis_index_groups=ring)
    dx, slope, xw, gw, dbc, slope2, row = call(
        inner_body,
        [
            far(SEG, HALF, dtype=BF16),
            far(SEG, HALF, dtype=BF16),
            far(SEG, HALF, dtype=BF16),
            far(SEG, HALF, dtype=BF16),
            far(SEG, 2 * LANES, dtype=BF16),
            far(SEG, 2 * LANES, dtype=BF16),
            far(3 * n, ROWS),
        ],
        [VMEM] * 6,
        ext,
    )(got, halo, taps, by_row, by_col, bc_act)
    scanned = call(scan_body, [shape(chips, 2 * ROWS, LANES, dtype=BF16)], [VMEM])(sent)[0]
    states = lax.all_to_all(scanned, "seq", 0, 0, axis_index_groups=ring)
    dpre, gstep, part = call(
        last_body,
        [kept(PAIRS + 2, SEG + 2 * HALO, LANES), far(n, ROWS), far(PAIRS, 8, LANES, dtype=BF16)],
        [VMEM] * 13 + [FAR] * 3,
        ext
        + [
            pltpu.VMEM((n, ROWS), F32),
            pltpu.VMEM((2, ROWS, HALF), BF16),
            pltpu.VMEM((2, ROWS, HALF), BF16),
            pltpu.VMEM((SEG, 2 * HALF), BF16),
            pltpu.VMEM((PAIRS, 8, LANES), F32),
        ],
    )(got, halo, by_row, by_col, parts, bc_act, side, states, near, dx, slope, xw, gw, dbc, slope2, row)
    part = lax.all_to_all(part, "seq", 0, 0, axis_index_groups=ring)
    part = spread(part, n_dp, 1.0)
    part = lax.all_to_all(part, "dp", 0, 0)
    part = spread(part, n_seq, 1.0 / n_dp)
    part = lax.all_to_all(part, "seq", 0, 0)
    gx, gbc, rim = call(
        input_body,
        [kept(SEG, HALF, dtype=BF16), kept(SEG, 2 * LANES), kept(PAIRS + 2, HALO, LANES, dtype=BF16)],
        [VMEM] * 2,
    )(dpre, taps)
    back = lax.ppermute(rim, "seq", [(i, i - 2) for i in range(2, n_seq)])
    keepx, keepbc, keepstep, give = call(
        swap_body,
        [
            kept(ROWS, HALF, dtype=BF16),
            kept(ROWS, 2 * LANES),
            kept(HEADS, ROWS),
            kept(PAIRS + 3, ROWS, LANES, dtype=BF16),
        ],
        [VMEM, VMEM, VMEM, FAR, VMEM],
    )(gx, gbc, back, gstep, side)
    came = lax.ppermute(give, "seq", [(i, i ^ 1) for i in range(n_seq)])
    gx, gbc, gstep = call(
        merge_body, [shape(ROWS, inner, dtype=BF16), shape(ROWS, 2 * LANES, dtype=BF16), shape(n, ROWS)], [VMEM] * 5
    )(keepx, keepbc, keepstep, came, side)
    weight, offset, bias, rate, skip = call(
        unpack_body,
        [shape(4, inner + 2 * LANES), shape(inner + 2 * LANES), shape(n), shape(n), shape(n)],
        [VMEM],
    )(part)
    return gx[None], gbc[None], gstep[None], weight, offset, bias, rate, skip


def solution(mesh):
    return jax.shard_map(
        compute,
        mesh=mesh,
        in_specs=(
            P("dp", "seq", None),
            P("dp", "seq", None),
            P("dp", None, "seq"),
            P(),
            P(),
            P(),
            P(),
            P(),
            P("dp", "seq", None),
        ),
        out_specs=(
            P("dp", "seq", None),
            P("dp", "seq", None),
            P("dp", None, "seq"),
            P(),
            P(),
            P(),
            P(),
            P(),
        ),
        check_vma=False,
    )
```
